32 devices in a mesh: ctx: 8 (over z, y), fsdp: 4 (over x, core).
Axes of the slice: x: 2, y: 2, z: 4, core: 2. Of those that a mesh axis runs over, the one named last changes fastest.
Arguments:
- tokens: bfloat16 [1024, 2048], P('ctx'), may hold values from -24 to 24
- positions: int32 [1024], replicated, may hold values from 0 to 1023, each once
- pulse_indicator: int32 [2, 1024, 2048], P(None, 'ctx'), may hold values 0 or 1
- norm_gain: float32 [2048], replicated, may hold values from 0.1 to 1.9
- in_weight: bfloat16 [2048, 3, 1024], P(None, None, 'fsdp'), may hold values from -0.375 to 0.375
- out_weight: bfloat16 [1024, 2048], P('fsdp'), may hold values from -0.1875 to 0.1875
- upstream: bfloat16 [1024, 2048], P('ctx'), may hold values from -6 to 6
Outputs:
- block_out: bfloat16 [1024, 2048], P('ctx', 'fsdp')
- token_grad: float32 [1024, 2048], P('ctx', 'fsdp')
- gain_grad: float32 [2048], P('fsdp')
- in_grad: float32 [2048, 3, 1024], P('ctx', None, 'fsdp')
- out_grad: float32 [2048, 1024], P('ctx', 'fsdp')
The draws below stay inside these ranges and needn't reach their ends.
Inputs may be any that keep to these rules, and one draw needn't show every extreme that they name: `positions`: each position of the sequence appears once.
All inputs are finite; a program needn't handle non-finite values. No bound on the sum of `pulse_indicator` on one device may be relied on, other than what follows from the above.
Results may differ from the reference program's by a relative error of at most 0.004.
The reference program's roundings to bfloat16 on the way (of `spikes`, `project`, `prob_low`, `attended`, `grad_attn`, `score_grad` and `grad_project`) count: a program that leaves them out, or rounds other values in their place, can miss the bound.
Values may be sent and summed in bfloat16 or wider, within the bound.
No kernel may reach another device: no remote copies, remote signals or barrier semaphores. Data moves between devices by JAX's collectives and lax.ppermute only.
A program may use at most 192 MiB of HBM per device.

```python
import math
import jax
import jax.numpy as jnp
from jax import lax

D = 2048
HEADS = 8
HEAD_DIM = 128
TIMESTEPS = 2
LEN = 1024


def draw_tokens(key, part):
    noise = jax.random.normal(key, (LEN, D), jnp.float32)
    column = jnp.exp(jnp.log(3.0) * jnp.arange(D, dtype=jnp.float32) / D)
    values = noise * column
    return jnp.clip(values, -24.0, 24.0).astype(jnp.bfloat16)


def plant(entries, stream_key, low, top_value):
    longest = entries.shape.index(max(entries.shape))
    spots = []
    for shift in (0, 1):
        where = [jax.random.randint(jax.random.fold_in(stream_key, axis), (), 0, length) for axis, length in enumerate(entries.shape)]
        where[longest] = (where[longest] + shift) % entries.shape[longest]
        spots.append(tuple(where))
    return entries.at[spots[0]].set(low).at[spots[1]].set(top_value)


def levels(key, shape, cuts, low, largest):
    level, own = 1.0, jax.random.fold_in(key, 6)
    for dim, shards_of in cuts:
        heights = jnp.exp(jax.random.uniform(jax.random.fold_in(own, dim), (shards_of,), jnp.float32, low / len(cuts), largest / len(cuts)))
        level = level * jnp.repeat(heights, shape[dim] // shards_of).reshape([-1 if axis == dim else 1 for axis in range(len(shape))])
    return level


def scatter_about(key, extent, width, bound, shards=(), kind=jnp.bfloat16):
    loudness = levels(key, extent, shards, -0.22, 0.18) if shards else 1.0
    array = jax.random.normal(key, extent, jnp.float32) * width * loudness
    return jnp.minimum(jnp.maximum(array, -bound), bound).astype(kind)


def setup_inputs(seed: int = 0) -> dict:
    seeds = jax.random.split(jax.random.key(seed), 8)
    tokens = draw_tokens(jax.random.fold_in(seeds[7], 71), 0)
    positions = jax.random.permutation(seeds[1], LEN).astype(jnp.int32)
    pulse_indicator = plant((jax.random.randint(seeds[2], (TIMESTEPS, LEN, D), 0, 2) < 1).astype(jnp.int32), jax.random.fold_in(seeds[2], 1), 0, 1)
    norm_gain = jnp.clip(1.0 + 0.18 * jax.random.normal(seeds[3], (D,), jnp.float32), 0.1, 1.9)
    in_weight = scatter_about(seeds[4], (D, 3, HEADS * HEAD_DIM), (D // 8) ** -0.5, 0.375, ((2, 4),))
    out_weight = scatter_about(seeds[5], (HEADS * HEAD_DIM, D), (HEADS * HEAD_DIM) ** -0.5, 0.1875, ((0, 4),))
    upstream = scatter_about(seeds[6], (LEN, D), 1.0, 6.0, ((0, 8),))
    return dict(tokens=tokens, positions=positions, pulse_indicator=pulse_indicator, norm_gain=norm_gain, in_weight=in_weight, out_weight=out_weight, upstream=upstream)


SOFT_CAP = 30.0
LEAK_RATE = 0.5
THRESHOLD = 1.0
SURROGATE_SLOPE = 4.0
EPSILON = 1e-05

def leaky_forward(tokens, pulse_indicator, norm_gain):
    values = tokens.astype(jnp.float32)
    inv_rms = lax.rsqrt(lax.optimization_barrier(jnp.mean(values * values, axis=-1, keepdims=True)) + EPSILON)
    normed = values * inv_rms
    current = normed * norm_gain
    neuron_voltage = current
    voltage_trace_record = []
    pulse_number_sum = jnp.zeros_like(current)
    for present_instant in range(TIMESTEPS):
        binary_pulses = pulse_indicator[present_instant].astype(jnp.float32)
        if present_instant > 0:
            neuron_voltage = LEAK_RATE * neuron_voltage * (1.0 - pulse_indicator[present_instant - 1].astype(jnp.float32)) + current
        voltage_trace_record.append(neuron_voltage)
        pulse_number_sum = pulse_number_sum + binary_pulses * neuron_voltage
    return (inv_rms, normed, voltage_trace_record, (pulse_number_sum / TIMESTEPS).astype(jnp.bfloat16))

def leaky_backward(grad_rate, pulse_indicator, voltage_trace_record):
    rescaled_logits = grad_rate / TIMESTEPS
    leaky_level_prior = jnp.zeros_like(rescaled_logits)
    grad_current = jnp.zeros_like(rescaled_logits)
    for present_instant in reversed(range(TIMESTEPS)):
        binary_pulses = pulse_indicator[present_instant].astype(jnp.float32)
        capped_logits = jax.nn.sigmoid(SURROGATE_SLOPE * (voltage_trace_record[present_instant] - THRESHOLD))
        voltage_adjoint = rescaled_logits * (binary_pulses + voltage_trace_record[present_instant] * SURROGATE_SLOPE * capped_logits * (1.0 - capped_logits)) + leaky_level_prior
        grad_current = grad_current + voltage_adjoint
        if present_instant > 0:
            leaky_level_prior = LEAK_RATE * voltage_adjoint * (1.0 - pulse_indicator[present_instant - 1].astype(jnp.float32))
    return grad_current

def reference(tokens, positions, pulse_indicator, norm_gain, in_weight, out_weight, upstream):
    score_scale = HEAD_DIM ** (-0.5)
    inv_rms, normed, voltage_trace_record, spikes = leaky_forward(tokens, pulse_indicator, norm_gain)
    head_width = HEADS * HEAD_DIM
    flat_in = in_weight.reshape(D, 3 * head_width)
    project = jnp.dot(spikes, flat_in, preferred_element_type=jnp.float32).astype(jnp.bfloat16)
    project = project.reshape(LEN, 3, head_width)
    grad_attn = jnp.dot(upstream, out_weight.T, preferred_element_type=jnp.float32).astype(jnp.bfloat16)
    block_rows = math.gcd(LEN, 512)
    block_count = LEN // block_rows

    def split_heads(matrix):
        return matrix.reshape(LEN, HEADS, HEAD_DIM).transpose(1, 0, 2)

    def one_head(head_items):
        head_query, head_key, head_value, head_grad = head_items

        def visit(running, piece):
            grad_keys, grad_values = running
            query_block, grad_block, query_pos = piece
            scores = jnp.dot(query_block, head_key.T, preferred_element_type=jnp.float32) * score_scale
            squashed = jnp.tanh(scores / SOFT_CAP)
            exponent = jnp.where(positions[None, :] <= query_pos[:, None], jnp.exp(SOFT_CAP * squashed), 0.0)
            totals = lax.optimization_barrier(jnp.sum(exponent, axis=-1, keepdims=True))
            attn_prob = exponent / totals
            prob_low = attn_prob.astype(jnp.bfloat16)
            attended_block = jnp.dot(prob_low, head_value, preferred_element_type=jnp.float32).astype(jnp.bfloat16)
            grad_prob = jnp.dot(grad_block, head_value.T, preferred_element_type=jnp.float32)
            delta = lax.optimization_barrier(jnp.sum(attn_prob * grad_prob, axis=-1, keepdims=True))
            score_grad = (attn_prob * (grad_prob - delta) * (1.0 - squashed * squashed) * score_scale).astype(jnp.bfloat16)
            grad_query = jnp.dot(score_grad, head_key, preferred_element_type=jnp.float32)
            grad_keys = grad_keys + jnp.dot(score_grad.T, query_block, preferred_element_type=jnp.float32)
            grad_values = grad_values + jnp.dot(prob_low.T, grad_block, preferred_element_type=jnp.float32)
            return ((grad_keys, grad_values), (attended_block, grad_query))
        empty = jnp.zeros((LEN, HEAD_DIM), jnp.float32)
        pieces = (head_query.reshape(block_count, block_rows, HEAD_DIM), head_grad.reshape(block_count, block_rows, HEAD_DIM), positions.reshape(block_count, block_rows))
        (grad_keys, grad_values), (attended_blocks, grad_queries) = lax.scan(visit, (empty, empty), pieces)
        return (attended_blocks.reshape(LEN, HEAD_DIM), grad_queries.reshape(LEN, HEAD_DIM), grad_keys, grad_values)
    attended_heads, grad_query_heads, grad_key_heads, grad_value_heads = lax.map(one_head, (split_heads(project[:, 0]), split_heads(project[:, 1]), split_heads(project[:, 2]), split_heads(grad_attn)))

    def join_heads(stacked):
        return stacked.transpose(1, 0, 2).reshape(LEN, head_width)
    attended = join_heads(attended_heads)
    grad_project = jnp.stack([join_heads(grad_query_heads).astype(jnp.bfloat16), join_heads(grad_key_heads).astype(jnp.bfloat16), join_heads(grad_value_heads).astype(jnp.bfloat16)], axis=1)
    block_out = (tokens.astype(jnp.float32) + jnp.dot(attended, out_weight, preferred_element_type=jnp.float32)).astype(jnp.bfloat16)
    flat_grad = grad_project.reshape(LEN, 3 * head_width)
    grad_spikes = jnp.dot(flat_grad, flat_in.T, preferred_element_type=jnp.float32)
    grad_current = leaky_backward(grad_spikes, pulse_indicator, voltage_trace_record)
    scaled_grad = grad_current * norm_gain
    row_mean = lax.optimization_barrier(jnp.mean(scaled_grad * normed, axis=-1, keepdims=True))
    token_grad = upstream.astype(jnp.float32) + inv_rms * (scaled_grad - normed * row_mean)
    gain_grad = lax.optimization_barrier(jnp.sum(grad_current * normed, axis=0))
    in_grad = jnp.dot(spikes.T, flat_grad, preferred_element_type=jnp.float32).reshape(D, 3, head_width)
    out_grad = jnp.dot(upstream.T, attended, preferred_element_type=jnp.float32)
    return (block_out, token_grad, gain_grad, in_grad, out_grad)
```

```python
import functools

import jax
import jax.numpy as jnp
from jax import lax
from jax.experimental import pallas as pl
from jax.experimental.pallas import tpu as pltpu
from jax.sharding import PartitionSpec as P

HEAD_DIM = 128
SOFT_CAP = 30.0
LEAK_RATE = 0.5
THRESHOLD = 1.0
SURROGATE_SLOPE = 4.0
EPSILON = 1e-05
F32 = jnp.float32
BF16 = jnp.bfloat16
VMEM_LIMIT = 50 << 20
EXTRA_ROWS = 8


def dot(a, b, dims):
    return lax.dot_general(a, b, (dims, ((), ())), preferred_element_type=F32)


NN = ((1,), (0,))
NT = ((1,), (1,))
TN = ((0,), (0,))


def params():
    return pltpu.CompilerParams(vmem_limit_bytes=VMEM_LIMIT)


def project_kernel(
    tok_ref, pulse_ref, gain_ref, win_ref, up_ref, wout_ref, pay_ref, spikes_ref, inv_ref, acc_ref
):
    step = pl.program_id(0)
    width = spikes_ref.shape[1]
    local = win_ref.shape[2]

    @pl.when(step == 0)
    def _():
        values = tok_ref[...].astype(F32)
        inv_ref[...] = lax.rsqrt(jnp.mean(values * values, axis=-1, keepdims=True) + EPSILON)
        acc_ref[...] = jnp.zeros_like(acc_ref)

    at = pl.multiple_of(step * width, width)
    current = tok_ref[:, pl.ds(at, width)].astype(F32) * inv_ref[...] * gain_ref[...]
    first = pulse_ref[0].astype(F32)
    second = pulse_ref[1].astype(F32)
    later = LEAK_RATE * current * (1.0 - first) + current
    spikes = ((first * current + second * later) * 0.5).astype(BF16)
    spikes_ref[...] = spikes
    for part in range(3):
        acc_ref[:, part * local : (part + 1) * local] += dot(spikes, win_ref[part], NN)
    acc_ref[:, 3 * local :] += dot(up_ref[...], wout_ref[...], NT)

    @pl.when(step == pl.num_programs(0) - 1)
    def _():
        pay_ref[...] = acc_ref[...].astype(BF16)


def project(tokens, pulse, gain, win, upstream, wout):
    rows, model = tokens.shape
    local = wout.shape[0]
    width = 256
    return pl.pallas_call(
        project_kernel,
        grid=(model // width,),
        in_specs=[
            pl.BlockSpec((rows, model), lambda k: (0, 0)),
            pl.BlockSpec((2, rows, width), lambda k: (0, 0, k)),
            pl.BlockSpec((1, width), lambda k: (0, k)),
            pl.BlockSpec((3, width, local), lambda k: (0, k, 0)),
            pl.BlockSpec((rows, width), lambda k: (0, k)),
            pl.BlockSpec((local, width), lambda k: (0, k)),
        ],
        out_specs=[
            pl.BlockSpec((rows, 4 * local), lambda k: (0, 0)),
            pl.BlockSpec((rows, width), lambda k: (0, k)),
            pl.BlockSpec((rows, 1), lambda k: (0, 0)),
        ],
        out_shape=[
            jax.ShapeDtypeStruct((rows, 4 * local), BF16),
            jax.ShapeDtypeStruct((rows, model), BF16),
            jax.ShapeDtypeStruct((rows, 1), F32),
        ],
        scratch_shapes=[pltpu.VMEM((rows, 4 * local), F32)],
        compiler_params=params(),
        name="project",
    )(tokens, pulse, gain, win, upstream, wout)


def factor_kernel(tok_ref, pulse_ref, gain_ref, inv_ref, factor_ref):
    current = tok_ref[...].astype(F32) * inv_ref[...] * gain_ref[...]
    first = pulse_ref[0].astype(F32)
    second = pulse_ref[1].astype(F32)
    later = LEAK_RATE * current * (1.0 - first) + current

    def slope(fired, membrane):
        level = jax.nn.sigmoid(SURROGATE_SLOPE * (membrane - THRESHOLD))
        return fired + membrane * SURROGATE_SLOPE * level * (1.0 - level)

    carried = 1.0 + LEAK_RATE * (1.0 - first)
    factor_ref[...] = 0.5 * (slope(first, current) + slope(second, later) * carried)


def factors(tokens, pulse, gain, inv):
    rows, model = tokens.shape
    width = 512
    return pl.pallas_call(
        factor_kernel,
        grid=(model // width,),
        in_specs=[
            pl.BlockSpec((rows, width), lambda k: (0, k)),
            pl.BlockSpec((2, rows, width), lambda k: (0, 0, k)),
            pl.BlockSpec((1, width), lambda k: (0, k)),
            pl.BlockSpec((rows, 1), lambda k: (0, 0)),
        ],
        out_specs=pl.BlockSpec((rows, width), lambda k: (0, k)),
        out_shape=jax.ShapeDtypeStruct((rows, model), F32),
        compiler_params=params(),
        name="factors",
    )(tokens, pulse, gain, inv)


def attention_kernel(
    q_ref, k_ref, v_ref, do_ref, prow_ref, pcol_ref, out_ref, dk_ref, dv_ref
):
    step = pl.program_id(1)
    block = q_ref.shape[0]
    scale = HEAD_DIM**-0.5
    query, grad = q_ref[...], do_ref[...]
    keys, values = k_ref[...], v_ref[...]
    squashed = jnp.tanh(dot(query, keys, NT) * (scale / SOFT_CAP))
    exponent = jnp.where(prow_ref[...] <= pcol_ref[...], jnp.exp(SOFT_CAP * squashed), 0.0)
    prob = exponent * (1.0 / jnp.sum(exponent, axis=-1, keepdims=True))
    low = prob.astype(BF16)
    grad_prob = dot(grad, values, NT)
    delta = jnp.sum(prob * grad_prob, axis=-1, keepdims=True)
    score_grad = (prob * (grad_prob - delta) * ((1.0 - squashed * squashed) * scale)).astype(BF16)
    at = pl.multiple_of(step * block, block)
    out_ref[3, pl.ds(at, block), :] = dot(low, values, NN).astype(BF16)
    out_ref[0, pl.ds(at, block), :] = dot(score_grad, keys, NN).astype(BF16)
    key_part = dot(score_grad, query, TN)
    value_part = dot(low, grad, TN)

    @pl.when(step == 0)
    def _():
        dk_ref[...] = key_part
        dv_ref[...] = value_part

    @pl.when(step > 0)
    def _():
        dk_ref[...] += key_part
        dv_ref[...] += value_part

    @pl.when(step == pl.num_programs(1) - 1)
    def _():
        out_ref[1] = dk_ref[...].astype(BF16)
        out_ref[2] = dv_ref[...].astype(BF16)


def attention(gathered, positions):
    length, width = gathered.shape
    heads = width // (4 * HEAD_DIM)
    block = max(16, (256 * 1024) // length)
    whole = functools.partial(pl.BlockSpec, (length, HEAD_DIM))
    part = functools.partial(pl.BlockSpec, (block, HEAD_DIM))
    return pl.pallas_call(
        attention_kernel,
        grid=(heads, length // block),
        in_specs=[
            part(lambda h, i: (i, h)),
            whole(lambda h, i: (0, heads + h)),
            whole(lambda h, i: (0, 2 * heads + h)),
            part(lambda h, i: (i, 3 * heads + h)),
            pl.BlockSpec((1, length), lambda h, i: (0, 0)),
            pl.BlockSpec((block, 1), lambda h, i: (i, 0)),
        ],
        out_specs=pl.BlockSpec((4, length, HEAD_DIM), lambda h, i: (0, 0, h)),
        out_shape=jax.ShapeDtypeStruct((4, length, heads * HEAD_DIM), BF16),
        scratch_shapes=[pltpu.VMEM((length, HEAD_DIM), F32)] * 2,
        compiler_params=params(),
        name="attention",
    )(gathered, gathered, gathered, gathered, positions[None, :], positions[:, None])


def spread_kernel(
    at_ref, grad_ref, win_ref, tok_ref, gain_ref, inv_ref, factor_ref, out_ref, sums_ref
):
    step = pl.program_id(0)
    rows = grad_ref.shape[1]
    share = sum(dot(grad_ref[part], win_ref[part], NT) for part in range(3))
    weighted = share * factor_ref[...] * (tok_ref[...].astype(F32) * inv_ref[...])
    out_ref[0, :rows, :] = share
    out_ref[0, pl.ds(rows, EXTRA_ROWS), :] = jnp.broadcast_to(
        jnp.sum(weighted, axis=0, keepdims=True), (EXTRA_ROWS, share.shape[1])
    )
    mine = jnp.sum(weighted * gain_ref[...], axis=1, keepdims=True)

    @pl.when(step == 0)
    def _():
        sums_ref[...] = mine

    @pl.when(step > 0)
    def _():
        sums_ref[...] += mine


def spread(fsdp_rank, own_block, grads, win, tokens, gain, inv, factor):
    rows, model = tokens.shape
    local = grads.shape[2]
    blocks = 4
    width = model // blocks
    column = lambda k, at: (0, at[0] ^ k)
    return pl.pallas_call(
        spread_kernel,
        grid_spec=pltpu.PrefetchScalarGridSpec(
            num_scalar_prefetch=1,
            grid=(blocks,),
            in_specs=[
                pl.BlockSpec((3, rows, local), lambda k, at: (0, at[1], 0)),
                pl.BlockSpec((3, width, local), lambda k, at: (0, at[0] ^ k, 0)),
                pl.BlockSpec((rows, width), column),
                pl.BlockSpec((1, width), column),
                pl.BlockSpec((rows, 1), lambda k, at: (0, 0)),
                pl.BlockSpec((rows, width), column),
            ],
            out_specs=[
                pl.BlockSpec((1, rows + EXTRA_ROWS, width), lambda k, at: (k, 0, 0)),
                pl.BlockSpec((rows, 1), lambda k, at: (0, 0)),
            ],
        ),
        out_shape=[
            jax.ShapeDtypeStruct((blocks, rows + EXTRA_ROWS, width), F32),
            jax.ShapeDtypeStruct((rows, 1), F32),
        ],
        compiler_params=params(),
        name="spread",
    )(jnp.stack([fsdp_rank, own_block]), grads, win, tokens, gain, inv, factor)


def swap(value, axis, mask):
    count = lax.axis_size(axis)
    return lax.ppermute(value, axis, [(i, i ^ mask) for i in range(count)])


def scatter_sum(first, second, third, fourth):
    near = swap(jnp.stack([second, fourth]), "fsdp", 1)
    return first + near[0] + swap(third + near[1], "fsdp", 2)


def weight_kernel(at_ref, both_ref, grad_ref, in_ref, out_ref):
    step = pl.program_id(0)
    fired, wanted = both_ref[0, 0], both_ref[0, 1]
    parts = [dot(fired, grad_ref[part], TN) for part in range(3)]
    last = dot(wanted, grad_ref[3], TN)

    @pl.when(step == 0)
    def _():
        for part in range(3):
            in_ref[part] = parts[part]
        out_ref[...] = last

    @pl.when(step > 0)
    def _():
        for part in range(3):
            in_ref[part] += parts[part]
        out_ref[...] += last


def weight_grads(turn, both, grads):
    blocks, _, rows, features = both.shape
    local = grads.shape[2]
    return pl.pallas_call(
        weight_kernel,
        grid_spec=pltpu.PrefetchScalarGridSpec(
            num_scalar_prefetch=1,
            grid=(blocks,),
            in_specs=[
                pl.BlockSpec((1, 2, rows, features), lambda j, at: (at[0] ^ j, 0, 0, 0)),
                pl.BlockSpec((4, rows, local), lambda j, at: (0, j, 0)),
            ],
            out_specs=[
                pl.BlockSpec((3, features, local), lambda j, at: (0, 0, 0)),
                pl.BlockSpec((features, local), lambda j, at: (0, 0)),
            ],
        ),
        out_shape=[
            jax.ShapeDtypeStruct((3, features, local), F32),
            jax.ShapeDtypeStruct((features, local), F32),
        ],
        compiler_params=params(),
        name="weight_grads",
    )(turn[None], both, grads)


def body(tokens, positions, pulse_indicator, norm_gain, in_weight, out_weight, upstream):
    ctx, fsdp = lax.axis_size("ctx"), lax.axis_size("fsdp")
    ctx_rank, fsdp_rank = lax.axis_index("ctx"), lax.axis_index("fsdp")
    rows, model = tokens.shape
    local = out_weight.shape[0]
    share = model // fsdp
    gain = norm_gain[None, :]
    win = jnp.transpose(in_weight, (1, 0, 2))
    payload, spikes, inv = project(tokens, pulse_indicator, gain, win, upstream, out_weight)
    factor = factors(tokens, pulse_indicator, gain, inv)

    if ctx == 8:
        turn = ctx_rank
        line = [payload] + [swap(payload, "ctx", 2 * step) for step in (1, 2, 3)]
        far = [swap(piece, "ctx", 1) for piece in line]
        blocks = [piece for pair in zip(line, far) for piece in pair]
        gathered = jnp.concatenate(blocks, axis=0)
        placed = jnp.concatenate(
            [lax.dynamic_slice_in_dim(positions, (turn ^ j) * rows, rows) for j in range(ctx)]
        )
    else:
        turn = jnp.zeros_like(ctx_rank)
        gathered = lax.all_gather(payload, "ctx", axis=0, tiled=True)
        placed = positions
    own = ctx_rank ^ turn
    grads = attention(gathered, placed)
    own_grads = lax.dynamic_slice_in_dim(grads, own * rows, rows, 1)

    spread_out, row_sums = spread(fsdp_rank, own, grads, win, tokens, gain, inv, factor)
    summed = scatter_sum(*(spread_out[j] for j in range(4)))
    row_mean = row_sums + swap(row_sums, "fsdp", 1)
    row_mean = (row_mean + swap(row_mean, "fsdp", 2)) / model
    low = fsdp_rank * share

    def columns(array):
        return lax.dynamic_slice_in_dim(array, low, share, 1)

    token_share = columns(tokens).astype(F32)
    scaled_grad = columns(factor) * summed[:rows] * columns(gain)
    token_grad = columns(upstream).astype(F32) + inv * (
        scaled_grad - token_share * inv * row_mean
    )
    gain_grad = summed[rows]
    if ctx == 8:
        for mask in (1, 2, 4):
            gain_grad = gain_grad + swap(gain_grad, "ctx", mask)
    else:
        gain_grad = lax.psum(gain_grad, "ctx")

    partial_out = jnp.dot(own_grads[3], out_weight, preferred_element_type=F32)
    pieces = [
        lax.dynamic_slice_in_dim(partial_out, (fsdp_rank ^ j) * share, share, 1) for j in range(4)
    ]
    block_out = (token_share + scatter_sum(*pieces)).astype(BF16)

    features = model // ctx

    both = jnp.stack([spikes, upstream]).reshape(2, rows, ctx, features)
    both = lax.all_to_all(both, "ctx", 2, 0)
    if features % 128 == 0:
        in_grad, out_grad = weight_grads(turn, both, grads)
    else:
        fired, wanted = (both[:, k].reshape(ctx * rows, features) for k in range(2))
        in_grad = jnp.stack([dot(fired, grads[part], TN) for part in range(3)])
        out_grad = dot(wanted, grads[3], TN)
    in_grad = jnp.transpose(in_grad, (1, 0, 2))
    return (block_out, token_grad, gain_grad, in_grad, out_grad)


def solution(mesh):
    placed = (
        P("ctx", None),
        P(),
        P(None, "ctx", None),
        P(),
        P(None, None, "fsdp"),
        P("fsdp", None),
        P("ctx", None),
    )
    return jax.shard_map(
        body,
        mesh=mesh,
        in_specs=placed,
        out_specs=(
            P("ctx", "fsdp"),
            P("ctx", "fsdp"),
            P("fsdp"),
            P("ctx", None, "fsdp"),
            P("ctx", "fsdp"),
        ),
        check_vma=False,
    )
```

```python
import functools

import jax
import jax.numpy as jnp
from jax import lax
from jax.experimental import pallas as pl
from jax.experimental.pallas import tpu as pltpu
from jax.sharding import PartitionSpec as P

HEAD_DIM = 128
SOFT_CAP = 30.0
LEAK_RATE = 0.5
THRESHOLD = 1.0
SURROGATE_SLOPE = 4.0
EPSILON = 1e-05
SUM_ROWS = 8
LOG2_E = 1.4426950408889634
F32 = jnp.float32
BF16 = jnp.bfloat16


def dot(a, b, dims):
    return lax.dot_general(a, b, (dims, ((), ())), preferred_element_type=F32)


NN = ((1,), (0,))
NT = ((1,), (1,))
TN = ((0,), (0,))


def params(mebibytes=50):
    return pltpu.CompilerParams(vmem_limit_bytes=mebibytes << 20)


def project_kernel(
    tok_hbm, pulse_hbm, gain_hbm, win_hbm, up_hbm, wout_hbm, pay_ref, spikes_ref, inv_ref,
    tok_ref, pulse_ref, gain_ref, win_ref, up_ref, wout_ref, acc_ref, sems, block_sems,
):
    model = tok_ref.shape[1]
    local = wout_ref.shape[0]
    blocks = block_sems.shape[0]
    width = model // blocks
    whole = [
        pltpu.make_async_copy(source, target, sems.at[k])
        for k, (source, target) in enumerate(
            [(tok_hbm, tok_ref), (gain_hbm, gain_ref), (up_hbm, up_ref), (wout_hbm, wout_ref)]
        )
    ]
    pairs = []
    for k in range(blocks):
        here = pl.ds(k * width, width)
        pulse = (pulse_hbm.at[:, :, here], pulse_ref.at[:, :, here])
        weight = (win_hbm.at[:, here, :], win_ref.at[:, here, :])
        pairs.append(
            [
                pltpu.make_async_copy(*ends, block_sems.at[k, n])
                for n, ends in enumerate((pulse, weight))
            ]
        )
    for copy in whole:
        copy.start()
    for pair in pairs:
        for copy in pair:
            copy.start()
    whole[0].wait()
    values = tok_ref[...].astype(F32)
    inv = lax.rsqrt(jnp.mean(values * values, axis=-1, keepdims=True) + EPSILON)
    inv_ref[...] = inv
    for copy in whole[1:]:
        copy.wait()
    pay_ref[:, 3 * local :] = dot(up_ref[...], wout_ref[...], NT).astype(BF16)
    for k, pair in enumerate(pairs):
        here = slice(k * width, (k + 1) * width)
        pair[0].wait()
        current = tok_ref[:, here].astype(F32) * inv * gain_ref[:, here]
        first = pulse_ref[0, :, here].astype(F32)
        second = pulse_ref[1, :, here].astype(F32)
        later = LEAK_RATE * current * (1.0 - first) + current
        spikes = ((first * current + second * later) * 0.5).astype(BF16)
        spikes_ref[:, here] = spikes
        pair[1].wait()
        for part in range(3):
            columns = slice(part * local, (part + 1) * local)
            share = dot(spikes, win_ref[part, here, :], NN)
            acc_ref[:, columns] = share if k == 0 else acc_ref[:, columns] + share
    pay_ref[:, : 3 * local] = acc_ref[...].astype(BF16)


def project(tokens, pulse, gain, win, upstream, wout):
    rows, model = tokens.shape
    local = wout.shape[0]
    blocks = 4
    arrays = (tokens, pulse, gain, win, upstream, wout)
    in_vmem = pl.BlockSpec(memory_space=pltpu.VMEM)
    return pl.pallas_call(
        project_kernel,
        in_specs=[pl.BlockSpec(memory_space=pltpu.HBM)] * 6,
        out_specs=[in_vmem] * 3,
        out_shape=[
            jax.ShapeDtypeStruct((rows, 4 * local), BF16),
            jax.ShapeDtypeStruct((rows, model), BF16),
            jax.ShapeDtypeStruct((rows, 1), F32),
        ],
        scratch_shapes=[pltpu.VMEM(array.shape, array.dtype) for array in arrays]
        + [
            pltpu.VMEM((rows, 3 * local), F32),
            pltpu.SemaphoreType.DMA((4,)),
            pltpu.SemaphoreType.DMA((blocks, 2)),
        ],
        compiler_params=params(24),
        name="project",
    )(*(pltpu.with_memory_space_constraint(array, pltpu.HBM) for array in arrays))


def factor_kernel(
    at_ref, tok_ref, pulse_ref, gain_ref, inv_ref, up_ref, factor_ref, rise_ref, fall_ref, base_ref, own_ref
):
    model = tok_ref.shape[1]
    width = own_ref.shape[1]
    inv, gain = inv_ref[...], gain_ref[...]
    current = tok_ref[...].astype(F32) * inv * gain
    first = pulse_ref[0].astype(F32)
    second = pulse_ref[1].astype(F32)
    later = LEAK_RATE * current * (1.0 - first) + current

    def slope(fired, membrane):
        level = jax.nn.sigmoid(SURROGATE_SLOPE * (membrane - THRESHOLD))
        return fired + membrane * SURROGATE_SLOPE * level * (1.0 - level)

    carried = 1.0 + LEAK_RATE * (1.0 - first)
    factor_ref[...] = 0.5 * (slope(first, current) + slope(second, later) * carried)
    here = pl.ds(pl.multiple_of(at_ref[0] * width, width), width)
    own = tok_ref[:, here].astype(F32)
    own_ref[...] = own
    base_ref[...] = up_ref[:, here].astype(F32)
    rise_ref[...] = factor_ref[:, here] * gain_ref[:, here] * inv
    fall_ref[...] = own * inv * (inv / model)


def factors(fsdp_rank, tokens, pulse, gain, inv, upstream, share):
    rows, model = tokens.shape
    in_vmem = pl.BlockSpec(memory_space=pltpu.VMEM)
    return pl.pallas_call(
        factor_kernel,
        in_specs=[pl.BlockSpec(memory_space=pltpu.SMEM)] + [in_vmem] * 5,
        out_specs=[in_vmem] * 5,
        out_shape=[jax.ShapeDtypeStruct((rows, model), F32)]
        + [jax.ShapeDtypeStruct((rows, share), F32)] * 4,
        compiler_params=params(24),
        name="factors",
    )(fsdp_rank[None], tokens, pulse, gain, inv, upstream)


def after(value, *others):
    return lax.optimization_barrier((value, others))[0]


def attend(query, keys, values, grad, allowed):
    scale = HEAD_DIM**-0.5
    squashed = jnp.tanh(dot(query, keys, NT) * (scale / SOFT_CAP))
    exponent = jnp.where(allowed, jnp.exp2((SOFT_CAP * LOG2_E) * squashed), 0.0)
    prob = exponent * (1.0 / jnp.sum(exponent, axis=-1, keepdims=True))
    low = prob.astype(BF16)
    grad_prob = dot(grad, values, NT)
    delta = jnp.sum(prob * grad_prob, axis=-1, keepdims=True)
    score_grad = (prob * (grad_prob - delta) * ((1.0 - squashed * squashed) * scale)).astype(BF16)
    attended = dot(low, values, NN).astype(BF16)
    grad_query = dot(score_grad, keys, NN).astype(BF16)
    return attended, grad_query, dot(score_grad, query, TN), dot(low, grad, TN)


def attention_kernel(*refs):
    *piece_refs, prow_ref, pcol_ref, out_ref, all_ref, dk_ref, dv_ref = refs
    rows = piece_refs[0].shape[0]
    length, width = all_ref.shape
    local = width // 4
    block = length // 2
    for j, piece in enumerate(piece_refs):
        all_ref[j * rows : (j + 1) * rows, :] = piece[...]
    dk_ref[...] = jnp.zeros_like(dk_ref)
    dv_ref[...] = jnp.zeros_like(dv_ref)

    def visit(step, carry):
        at = pl.ds(pl.multiple_of(step * block, block), block)
        allowed = prow_ref[...] <= pcol_ref[at, :]
        for low in range(0, local, HEAD_DIM):
            query, keys, values, grad = (
                slice(part * local + low, part * local + low + HEAD_DIM) for part in range(4)
            )
            here = slice(low, low + HEAD_DIM)
            attended, grad_query, key_part, value_part = attend(
                all_ref[at, query], all_ref[:, keys], all_ref[:, values], all_ref[at, grad], allowed
            )
            out_ref[3, at, here] = attended
            out_ref[0, at, here] = grad_query
            dk_ref[:, here] += key_part
            dv_ref[:, here] += value_part
        return carry

    lax.fori_loop(0, length // block, visit, 0)
    out_ref[1] = dk_ref[...].astype(BF16)
    out_ref[2] = dv_ref[...].astype(BF16)


def attention(pieces, positions):
    rows, width = pieces[0].shape
    length, local = len(pieces) * rows, width // 4
    in_vmem = pl.BlockSpec(memory_space=pltpu.VMEM)
    return pl.pallas_call(
        attention_kernel,
        in_specs=[in_vmem] * (len(pieces) + 2),
        out_specs=in_vmem,
        out_shape=jax.ShapeDtypeStruct((4, length, local), BF16),
        scratch_shapes=[pltpu.VMEM((length, width), BF16)]
        + [pltpu.VMEM((length, local), F32)] * 2,
        compiler_params=params(36),
        name="attention",
    )(*pieces, positions[None, :], positions[:, None])


def long_kernel(q_ref, k_ref, v_ref, do_ref, prow_ref, pcol_ref, out_ref, dk_ref, dv_ref):
    step = pl.program_id(1)
    block = q_ref.shape[0]

    @pl.when(step == 0)
    def _():
        dk_ref[...] = jnp.zeros_like(dk_ref)
        dv_ref[...] = jnp.zeros_like(dv_ref)

    attended, grad_query, key_part, value_part = attend(
        q_ref[...], k_ref[...], v_ref[...], do_ref[...], prow_ref[...] <= pcol_ref[...]
    )
    at = pl.ds(pl.multiple_of(step * block, block), block)
    out_ref[3, at, :] = attended
    out_ref[0, at, :] = grad_query
    dk_ref[...] += key_part
    dv_ref[...] += value_part

    @pl.when(step == pl.num_programs(1) - 1)
    def _():
        out_ref[1] = dk_ref[...].astype(BF16)
        out_ref[2] = dv_ref[...].astype(BF16)


def long_attention(gathered, positions):
    length, width = gathered.shape
    heads = width // (4 * HEAD_DIM)
    block = max(16, (256 * 1024) // length)
    whole = functools.partial(pl.BlockSpec, (length, HEAD_DIM))
    part = functools.partial(pl.BlockSpec, (block, HEAD_DIM))
    return pl.pallas_call(
        long_kernel,
        grid=(heads, length // block),
        in_specs=[
            part(lambda h, i: (i, h)),
            whole(lambda h, i: (0, heads + h)),
            whole(lambda h, i: (0, 2 * heads + h)),
            part(lambda h, i: (i, 3 * heads + h)),
            pl.BlockSpec((1, length), lambda h, i: (0, 0)),
            pl.BlockSpec((block, 1), lambda h, i: (i, 0)),
        ],
        out_specs=pl.BlockSpec((4, length, HEAD_DIM), lambda h, i: (0, 0, h)),
        out_shape=jax.ShapeDtypeStruct((4, length, heads * HEAD_DIM), BF16),
        scratch_shapes=[pltpu.VMEM((length, HEAD_DIM), F32)] * 2,
        compiler_params=params(),
        name="long_attention",
    )(gathered, gathered, gathered, gathered, positions[None, :], positions[:, None])


def spread_kernel(
    at_ref, grad_ref, win_ref, wout_ref, tok_ref, gain_ref, inv_ref, factor_ref,
    own_ref, far_ref, near_ref, own_out_ref, far_out_ref, near_out_ref, gain_out_ref,
):
    rows = tok_ref.shape[0]
    width = own_ref.shape[1]
    sums = jnp.zeros((rows, 1), F32)
    targets = (own_ref, near_ref.at[1], far_ref, near_ref.at[0])
    out_targets = (own_out_ref, near_out_ref.at[1], far_out_ref, near_out_ref.at[0])
    for k in range(4):
        here = pl.ds(pl.multiple_of((at_ref[0] ^ k) * width, width), width)
        share = sum(dot(grad_ref[part], win_ref[part, here, :], NT) for part in range(3))
        targets[k][:rows, :] = share
        out_targets[k][...] = dot(grad_ref[3], wout_ref[:, here], NN)
        weighted = share * factor_ref[:, here] * (tok_ref[:, here].astype(F32) * inv_ref[...])
        gain_out_ref[k : k + 1, :] = jnp.sum(weighted, axis=0, keepdims=True)
        sums += jnp.sum(weighted * gain_ref[:, here], axis=1, keepdims=True)
    line = jnp.broadcast_to(sums, (rows, rows)).T[:SUM_ROWS, :]
    for target in targets:
        target[rows:, :] = jnp.broadcast_to(line[:, :1], (SUM_ROWS, width))
        target[rows:, :rows] = line


def spread(fsdp_rank, own_grads, win, wout, tokens, gain, inv, factor):
    rows, model = tokens.shape
    width = model // 4
    in_vmem = pl.BlockSpec(memory_space=pltpu.VMEM)
    tall = jax.ShapeDtypeStruct((rows + SUM_ROWS, width), F32)
    flat = jax.ShapeDtypeStruct((rows, width), F32)
    return pl.pallas_call(
        spread_kernel,
        in_specs=[pl.BlockSpec(memory_space=pltpu.SMEM)] + [in_vmem] * 7,
        out_specs=[in_vmem] * 7,
        out_shape=[
            tall,
            tall,
            jax.ShapeDtypeStruct((2,) + tall.shape, F32),
            flat,
            flat,
            jax.ShapeDtypeStruct((2,) + flat.shape, F32),
            jax.ShapeDtypeStruct((4, width), F32),
        ],
        compiler_params=params(24),
        name="spread",
    )(fsdp_rank[None], own_grads, win, wout, tokens, gain, inv, factor)


def swap(value, axis, mask):
    count = lax.axis_size(axis)
    return lax.ppermute(value, axis, [(i, i ^ mask) for i in range(count)])


def weight_kernel(at_ref, *refs):
    *piece_refs, grad_ref, in_ref, out_ref, both_ref = refs
    ranks, rows, width = piece_refs[0].shape
    features = width // 2
    for k, piece in enumerate(piece_refs):
        for j in range(ranks):
            low = (j * len(piece_refs) + (at_ref[0] ^ k)) * rows
            both_ref[pl.ds(pl.multiple_of(low, rows), rows), :] = piece[at_ref[1] ^ j]
    fired, wanted = both_ref[:, :features], both_ref[:, features:]
    for part in range(3):
        in_ref[part] = dot(fired, grad_ref[part], TN)
    out_ref[...] = dot(wanted, grad_ref[3], TN)


def weight_grads(fsdp_rank, turn, pieces, grads):
    features = pieces[0].shape[2] // 2
    local = grads.shape[2]
    in_vmem = pl.BlockSpec(memory_space=pltpu.VMEM)
    return pl.pallas_call(
        weight_kernel,
        in_specs=[pl.BlockSpec(memory_space=pltpu.SMEM)] + [in_vmem] * (len(pieces) + 1),
        out_specs=[in_vmem, in_vmem],
        out_shape=[
            jax.ShapeDtypeStruct((3, features, local), F32),
            jax.ShapeDtypeStruct((features, local), F32),
        ],
        scratch_shapes=[pltpu.VMEM((grads.shape[1], 2 * features), BF16)],
        compiler_params=params(),
        name="weight_grads",
    )(jnp.stack([fsdp_rank, turn]), *pieces, grads)


def body(tokens, positions, pulse_indicator, norm_gain, in_weight, out_weight, upstream):
    ctx, fsdp = lax.axis_size("ctx"), lax.axis_size("fsdp")
    ctx_rank, fsdp_rank = lax.axis_index("ctx"), lax.axis_index("fsdp")
    rows, model = tokens.shape
    local = out_weight.shape[0]
    share = model // fsdp
    gain = norm_gain[None, :]
    features = model // ctx
    win = jnp.transpose(in_weight, (1, 0, 2))
    payload, spikes, inv = project(tokens, pulse_indicator, gain, win, upstream, out_weight)
    factor, rise, fall, base, token_share = factors(
        fsdp_rank, tokens, pulse_indicator, gain, inv, upstream, share
    )

    short = ctx == 8 and fsdp == 4
    if short:
        beside = swap(payload, "ctx", 2)
        below = swap(payload, "ctx", 1)
        across = swap(payload, "ctx", 4)
        blocks = [payload, below, beside, swap(beside, "ctx", 1), across, swap(across, "ctx", 1)]
        corner = swap(across, "ctx", 2)
        blocks += [corner, swap(corner, "ctx", 1)]
        placed = jnp.concatenate(
            [lax.dynamic_slice_in_dim(positions, (ctx_rank ^ j) * rows, rows) for j in range(ctx)]
        )
        quarter = rows // fsdp
        both = jnp.stack([spikes, upstream], axis=1)
        both = lax.dynamic_slice_in_dim(both, fsdp_rank * quarter, quarter, 0)
        both = both.reshape(quarter, 2, ctx, features).transpose(2, 0, 1, 3)
        both = after(both.reshape(ctx, quarter, 2 * features), below)
        both = lax.all_to_all(both, "ctx", 0, 0)
        over = swap(both, "fsdp", 2)
        pieces = [both, swap(both, "fsdp", 1), over, swap(over, "fsdp", 1)]
        grads = attention(blocks, after(placed, over))
        own_grads = grads[:, :rows]
        in_grad, out_grad = weight_grads(fsdp_rank, ctx_rank, pieces, grads)
    else:
        grads = long_attention(lax.all_gather(payload, "ctx", axis=0, tiled=True), positions)
        own_grads = lax.dynamic_slice_in_dim(grads, ctx_rank * rows, rows, 1)
        fired, wanted = (
            lax.all_to_all(array.reshape(rows, ctx, features), "ctx", 1, 0).reshape(-1, features)
            for array in (spikes, upstream)
        )
        in_grad = jnp.stack([dot(fired, grads[part], TN) for part in range(3)])
        out_grad = dot(wanted, grads[3], TN)

    own, far, near, own_out, far_out, near_out, gains = spread(
        fsdp_rank, own_grads, win, out_weight, tokens, gain, inv, factor
    )
    near = swap(near, "fsdp", 1)
    far = far + near[0]
    landed = swap(far, "fsdp", 2)
    near_out = swap(after(near_out, far), "fsdp", 1)
    landed_out = swap(far_out + near_out[0], "fsdp", 2)
    if short:
        gains = gains + swap(gains, "ctx", 1)
        gains = after(gains, far)
        for mask in (2, 4):
            gains = gains + swap(gains, "ctx", mask)
        landed = after(landed, in_grad, out_grad)
    else:
        gains = lax.psum(gains, "ctx")
    gain_near = swap(jnp.stack([gains[3], gains[1]]), "fsdp", 1)
    gain_grad = gains[0] + gain_near[1] + swap(gains[2] + gain_near[0], "fsdp", 2)

    grad_spikes = own + near[1] + landed
    token_grad = base + (rise * grad_spikes[:rows] - fall * grad_spikes[rows, :rows][:, None])
    block_out = (token_share + (own_out + near_out[1] + landed_out)).astype(BF16)
    return (block_out, token_grad, gain_grad, jnp.transpose(in_grad, (1, 0, 2)), out_grad)


def solution(mesh):
    placed = (
        P("ctx", None),
        P(),
        P(None, "ctx", None),
        P(),
        P(None, None, "fsdp"),
        P("fsdp", None),
        P("ctx", None),
    )
    return jax.shard_map(
        body,
        mesh=mesh,
        in_specs=placed,
        out_specs=(
            P("ctx", "fsdp"),
            P("ctx", "fsdp"),
            P("fsdp"),
            P("ctx", None, "fsdp"),
            P("ctx", "fsdp"),
        ),
        check_vma=False,
    )
```

```python
import functools

import jax
import jax.numpy as jnp
from jax import lax
from jax.experimental import pallas as pl
from jax.experimental.pallas import tpu as pltpu
from jax.sharding import PartitionSpec as P

HEAD_DIM = 128
SOFT_CAP = 30.0
LEAK_RATE = 0.5
THRESHOLD = 1.0
SURRO4_SLOPE = 4.0
EPSILON = 1e-05
SUM_ROWS = 8
LOG2_E = 1.4426950408889634
F32 = jnp.float32
BF16 = jnp.bfloat16


def dot(a, b, dims):
    return lax.dot_general(a, b, (dims, ((), ())), preferred_element_type=F32)


NN = ((1,), (0,))
NT = ((1,), (1,))
TN = ((0,), (0,))


def params(mebibytes=50):
    return pltpu.CompilerParams(vmem_limit_bytes=mebibytes << 20)


def project_kernel(
    at_ref, tok_hbm, pulse_hbm, gain_hbm, win_hbm, up_hbm, wout_hbm, pay_ref, spikes_ref, inv_ref, send_ref,
    tok_ref, pulse_ref, gain_ref, win_ref, up_ref, wout_ref, acc_ref, sems, block_sems,
):
    model = tok_ref.shape[1]
    local = wout_ref.shape[0]
    blocks = block_sems.shape[0]
    width = model // blocks
    ends = [(tok_hbm, tok_ref), (gain_hbm, gain_ref), (up_hbm, up_ref), (wout_hbm, wout_ref)]
    whole = [pltpu.make_async_copy(*pair, sems.at[k]) for k, pair in enumerate(ends)]
    pairs = []
    for k in range(blocks):
        here = pl.ds(k * width, width)
        pulse = (pulse_hbm.at[:, :, here], pulse_ref.at[:, :, here])
        weight = (win_hbm.at[:, here, :], win_ref.at[:, here, :])
        pairs.append(
            [
                pltpu.make_async_copy(*pair, block_sems.at[k, n])
                for n, pair in enumerate((pulse, weight))
            ]
        )
    for copy in [*whole[:2], *(copy for pair in pairs for copy in pair), *whole[2:]]:
        copy.start()
    whole[0].wait()
    values = tok_ref[...].astype(F32)
    inv = lax.rsqrt(jnp.mean(values * values, axis=-1, keepdims=True) + EPSILON)
    inv_ref[...] = inv
    whole[1].wait()
    for k, pair in enumerate(pairs):
        here = slice(k * width, (k + 1) * width)
        pair[0].wait()
        current = tok_ref[:, here].astype(F32) * inv * gain_ref[:, here]
        first = pulse_ref[0, :, here].astype(F32)
        second = pulse_ref[1, :, here].astype(F32)
        later = LEAK_RATE * current * (1.0 - first) + current
        spikes = ((first * current + second * later) * 0.5).astype(BF16)
        spikes_ref[:, here] = spikes
        pair[1].wait()
        for part in range(3):
            columns = slice(part * local, (part + 1) * local)
            share = dot(spikes, win_ref[part, here, :], NN)
            acc_ref[:, columns] = share if k == 0 else acc_ref[:, columns] + share
    pay_ref[:, : 3 * local] = acc_ref[...].astype(BF16)
    for copy in whole[2:]:
        copy.wait()
    pay_ref[:, 3 * local :] = dot(up_ref[...], wout_ref[...], NT).astype(BF16)
    ranks, quarter, both = send_ref.shape
    features = both // 2
    mine = pl.ds(pl.multiple_of(at_ref[0] * quarter, quarter), quarter)
    for rank in range(ranks):
        here = slice(rank * features, (rank + 1) * features)
        send_ref[rank, :, :features] = spikes_ref[mine, here]
        send_ref[rank, :, features:] = up_ref[mine, here]


def project(fsdp_rank, ctx, tokens, pulse, gain, win, upstream, wout):
    rows, model = tokens.shape
    local = wout.shape[0]
    blocks = 4
    arrays = (tokens, pulse, gain, win, upstream, wout)
    in_vmem = pl.BlockSpec(memory_space=pltpu.VMEM)
    return pl.pallas_call(
        project_kernel,
        in_specs=[pl.BlockSpec(memory_space=pltpu.SMEM)]
        + [pl.BlockSpec(memory_space=pltpu.HBM)] * 6,
        out_specs=[in_vmem] * 4,
        out_shape=[
            jax.ShapeDtypeStruct((rows, 4 * local), BF16),
            jax.ShapeDtypeStruct((rows, model), BF16),
            jax.ShapeDtypeStruct((rows, 1), F32),
            jax.ShapeDtypeStruct((ctx, rows // 4, 2 * (model // ctx)), BF16),
        ],
        scratch_shapes=[pltpu.VMEM(array.shape, array.dtype) for array in arrays]
        + [
            pltpu.VMEM((rows, 3 * local), F32),
            pltpu.SemaphoreType.DMA((4,)),
            pltpu.SemaphoreType.DMA((blocks, 2)),
        ],
        compiler_params=params(24),
        name="project",
    )(
        fsdp_rank[None],
        *(pltpu.with_memory_space_constraint(array, pltpu.HBM) for array in arrays),
    )


def factor_kernel(
    at_ref, tok_ref, pulse_ref, gain_ref, inv_ref, up_ref, factor_ref, rise_ref, fall_ref, base_ref, own_ref
):
    model = tok_ref.shape[1]
    width = own_ref.shape[1]
    inv, gain = inv_ref[...], gain_ref[...]
    current = tok_ref[...].astype(F32) * inv * gain
    first = pulse_ref[0].astype(F32)
    second = pulse_ref[1].astype(F32)
    later = LEAK_RATE * current * (1.0 - first) + current

    def slope(fired, membrane):
        level = jax.nn.sigmoid(SURRO4_SLOPE * (membrane - THRESHOLD))
        return fired + membrane * SURRO4_SLOPE * level * (1.0 - level)

    carried = 1.0 + LEAK_RATE * (1.0 - first)
    factor_ref[...] = 0.5 * (slope(first, current) + slope(second, later) * carried)
    here = pl.ds(pl.multiple_of(at_ref[0] * width, width), width)
    own = tok_ref[:, here].astype(F32)
    own_ref[...] = own
    base_ref[...] = up_ref[:, here].astype(F32)
    rise_ref[...] = factor_ref[:, here] * gain_ref[:, here] * inv
    fall_ref[...] = own * inv * (inv / model)


def factors(fsdp_rank, tokens, pulse, gain, inv, upstream, share):
    rows, model = tokens.shape
    in_vmem = pl.BlockSpec(memory_space=pltpu.VMEM)
    return pl.pallas_call(
        factor_kernel,
        in_specs=[pl.BlockSpec(memory_space=pltpu.SMEM)] + [in_vmem] * 5,
        out_specs=[in_vmem] * 5,
        out_shape=[jax.ShapeDtypeStruct((rows, model), F32)]
        + [jax.ShapeDtypeStruct((rows, share), F32)] * 4,
        compiler_params=params(24),
        name="factors",
    )(fsdp_rank[None], tokens, pulse, gain, inv, upstream)


def after(value, *others):
    return lax.optimization_barrier((value, others))[0]


def attend(query, keys, values, grad, allowed):
    scale = HEAD_DIM**-0.5
    squashed = jnp.tanh(dot(query, keys, NT) * (scale / SOFT_CAP))
    exponent = jnp.where(allowed, jnp.exp2((SOFT_CAP * LOG2_E) * squashed), 0.0)
    prob = exponent * (1.0 / jnp.sum(exponent, axis=-1, keepdims=True))
    low = prob.astype(BF16)
    grad_prob = dot(grad, values, NT)
    delta = jnp.sum(prob * grad_prob, axis=-1, keepdims=True)
    score_grad = (prob * (grad_prob - delta) * ((1.0 - squashed * squashed) * scale)).astype(BF16)
    attended = dot(low, values, NN).astype(BF16)
    grad_query = dot(score_grad, keys, NN).astype(BF16)
    return attended, grad_query, dot(score_grad, query, TN), dot(low, grad, TN)


def attention_kernel(*refs):
    *piece_refs, prow_ref, pcol_ref, out_ref, all_ref, dk_ref, dv_ref = refs
    rows = piece_refs[0].shape[0]
    length, width = all_ref.shape
    local = width // 4
    block = length // 2
    for j, piece in enumerate(piece_refs):
        all_ref[j * rows : (j + 1) * rows, :] = piece[...]
    dk_ref[...] = jnp.zeros_like(dk_ref)
    dv_ref[...] = jnp.zeros_like(dv_ref)

    def visit(step, carry):
        at = pl.ds(pl.multiple_of(step * block, block), block)
        allowed = prow_ref[...] <= pcol_ref[at, :]
        for low in range(0, local, HEAD_DIM):
            query, keys, values, grad = (
                slice(part * local + low, part * local + low + HEAD_DIM) for part in range(4)
            )
            here = slice(low, low + HEAD_DIM)
            attended, grad_query, key_part, value_part = attend(
                all_ref[at, query], all_ref[:, keys], all_ref[:, values], all_ref[at, grad], allowed
            )
            out_ref[3, at, here] = attended
            out_ref[0, at, here] = grad_query
            dk_ref[:, here] += key_part
            dv_ref[:, here] += value_part
        return carry

    lax.fori_loop(0, length // block, visit, 0)
    out_ref[1] = dk_ref[...].astype(BF16)
    out_ref[2] = dv_ref[...].astype(BF16)


def attention(pieces, positions):
    rows, width = pieces[0].shape
    length, local = len(pieces) * rows, width // 4
    in_vmem = pl.BlockSpec(memory_space=pltpu.VMEM)
    return pl.pallas_call(
        attention_kernel,
        in_specs=[in_vmem] * (len(pieces) + 2),
        out_specs=in_vmem,
        out_shape=jax.ShapeDtypeStruct((4, length, local), BF16),
        scratch_shapes=[pltpu.VMEM((length, width), BF16)]
        + [pltpu.VMEM((length, local), F32)] * 2,
        compiler_params=params(36),
        name="attention",
    )(*pieces, positions[None, :], positions[:, None])


def long_kernel(q_ref, k_ref, v_ref, do_ref, prow_ref, pcol_ref, out_ref, dk_ref, dv_ref):
    step = pl.program_id(1)
    block = q_ref.shape[0]

    @pl.when(step == 0)
    def _():
        dk_ref[...] = jnp.zeros_like(dk_ref)
        dv_ref[...] = jnp.zeros_like(dv_ref)

    attended, grad_query, key_part, value_part = attend(
        q_ref[...], k_ref[...], v_ref[...], do_ref[...], prow_ref[...] <= pcol_ref[...]
    )
    at = pl.ds(pl.multiple_of(step * block, block), block)
    out_ref[3, at, :] = attended
    out_ref[0, at, :] = grad_query
    dk_ref[...] += key_part
    dv_ref[...] += value_part

    @pl.when(step == pl.num_programs(1) - 1)
    def _():
        out_ref[1] = dk_ref[...].astype(BF16)
        out_ref[2] = dv_ref[...].astype(BF16)


def long_attention(gathered, positions):
    length, width = gathered.shape
    heads = width // (4 * HEAD_DIM)
    block = max(16, (256 * 1024) // length)
    whole = functools.partial(pl.BlockSpec, (length, HEAD_DIM))
    part = functools.partial(pl.BlockSpec, (block, HEAD_DIM))
    return pl.pallas_call(
        long_kernel,
        grid=(heads, length // block),
        in_specs=[
            part(lambda h, i: (i, h)),
            whole(lambda h, i: (0, heads + h)),
            whole(lambda h, i: (0, 2 * heads + h)),
            part(lambda h, i: (i, 3 * heads + h)),
            pl.BlockSpec((1, length), lambda h, i: (0, 0)),
            pl.BlockSpec((block, 1), lambda h, i: (i, 0)),
        ],
        out_specs=pl.BlockSpec((4, length, HEAD_DIM), lambda h, i: (0, 0, h)),
        out_shape=jax.ShapeDtypeStruct((4, length, heads * HEAD_DIM), BF16),
        scratch_shapes=[pltpu.VMEM((length, HEAD_DIM), F32)] * 2,
        compiler_params=params(),
        name="long_attention",
    )(gathered, gathered, gathered, gathered, positions[None, :], positions[:, None])


def spread_kernel(
    at_ref, grad_ref, win_ref, wout_ref, tok_ref, gain_ref, inv_ref, factor_ref,
    own_ref, far_ref, near_ref,
):
    rows = tok_ref.shape[0]
    width = own_ref.shape[1]
    below = rows + SUM_ROWS
    sums = jnp.zeros((rows, 1), F32)
    targets = (own_ref, near_ref.at[1], far_ref, near_ref.at[0])
    for k in range(4):
        here = pl.ds(pl.multiple_of((at_ref[0] ^ k) * width, width), width)
        share = sum(dot(grad_ref[part], win_ref[part, here, :], NT) for part in range(3))
        targets[k][:rows, :] = share
        targets[k][below:, :] = dot(grad_ref[3], wout_ref[:, here], NN)
        weighted = share * factor_ref[:, here] * (tok_ref[:, here].astype(F32) * inv_ref[...])
        targets[k][rows:below, :] = jnp.broadcast_to(
            jnp.sum(weighted, axis=0, keepdims=True), (SUM_ROWS, width)
        )
        sums += jnp.sum(weighted * gain_ref[:, here], axis=1, keepdims=True)
    line = jnp.broadcast_to(sums, (rows, rows)).T[:1, :]
    for target in targets:
        target[rows : rows + 1, :rows] = line


def spread(fsdp_rank, own_grads, win, wout, tokens, gain, inv, factor):
    rows, model = tokens.shape
    width = model // 4
    in_vmem = pl.BlockSpec(memory_space=pltpu.VMEM)
    tall = (2 * rows + SUM_ROWS, width)
    return pl.pallas_call(
        spread_kernel,
        in_specs=[pl.BlockSpec(memory_space=pltpu.SMEM)] + [in_vmem] * 7,
        out_specs=[in_vmem] * 3,
        out_shape=[
            jax.ShapeDtypeStruct(tall, F32),
            jax.ShapeDtypeStruct(tall, F32),
            jax.ShapeDtypeStruct((2,) + tall, F32),
        ],
        compiler_params=params(20),
        name="spread",
    )(fsdp_rank[None], own_grads, win, wout, tokens, gain, inv, factor)


def swap(value, axis, mask):
    count = lax.axis_size(axis)
    return lax.ppermute(value, axis, [(i, i ^ mask) for i in range(count)])


def weight_kernel(at_ref, *refs):
    *piece_refs, grad_ref, in_ref, out_ref, both_ref = refs
    ranks, rows, width = piece_refs[0].shape
    features = width // 2
    for k, piece in enumerate(piece_refs):
        for j in range(ranks):
            low = (j * len(piece_refs) + (at_ref[0] ^ k)) * rows
            both_ref[pl.ds(pl.multiple_of(low, rows), rows), :] = piece[at_ref[1] ^ j]
    fired, wanted = both_ref[:, :features], both_ref[:, features:]
    for part in range(3):
        in_ref[part] = dot(fired, grad_ref[part], TN)
    out_ref[...] = dot(wanted, grad_ref[3], TN)


def weight_grads(fsdp_rank, turn, pieces, grads):
    features = pieces[0].shape[2] // 2
    local = grads.shape[2]
    in_vmem = pl.BlockSpec(memory_space=pltpu.VMEM)
    return pl.pallas_call(
        weight_kernel,
        in_specs=[pl.BlockSpec(memory_space=pltpu.SMEM)] + [in_vmem] * (len(pieces) + 1),
        out_specs=[in_vmem, in_vmem],
        out_shape=[
            jax.ShapeDtypeStruct((3, features, local), F32),
            jax.ShapeDtypeStruct((features, local), F32),
        ],
        scratch_shapes=[pltpu.VMEM((grads.shape[1], 2 * features), BF16)],
        compiler_params=params(16),
        name="weight_grads",
    )(jnp.stack([fsdp_rank, turn]), *pieces, grads)


def body(tokens, positions, pulse_indicator, norm_gain, in_weight, out_weight, upstream):
    ctx, fsdp = lax.axis_size("ctx"), lax.axis_size("fsdp")
    ctx_rank, fsdp_rank = lax.axis_index("ctx"), lax.axis_index("fsdp")
    rows, model = tokens.shape
    local = out_weight.shape[0]
    share = model // fsdp
    gain = norm_gain[None, :]
    features = model // ctx
    win = jnp.transpose(in_weight, (1, 0, 2))
    payload, spikes, inv, both = project(
        fsdp_rank, ctx, tokens, pulse_indicator, gain, win, upstream, out_weight
    )
    factor, rise, fall, base, token_share = factors(
        fsdp_rank, tokens, pulse_indicator, gain, inv, upstream, share
    )

    short = ctx == 8 and fsdp == 4
    if short:
        beside = swap(payload, "ctx", 2)
        below = swap(payload, "ctx", 1)
        across = swap(payload, "ctx", 4)
        diagonal = swap(beside, "ctx", 1)
        corner = swap(across, "ctx", 2)
        across_below = swap(across, "ctx", 1)
        blocks = [payload, below, beside, diagonal, across, across_below]
        blocks += [corner, swap(corner, "ctx", 1)]
        placed = jnp.concatenate(
            [lax.dynamic_slice_in_dim(positions, (ctx_rank ^ j) * rows, rows) for j in range(ctx)]
        )
        both = lax.all_to_all(after(both, below), "ctx", 0, 0)
        over = swap(both, "fsdp", 2)
        pieces = [both, swap(both, "fsdp", 1), over, swap(over, "fsdp", 1)]
        grads = attention(blocks, after(placed, over))
        own_grads = grads[:, :rows]
        in_grad, out_grad = weight_grads(fsdp_rank, ctx_rank, pieces, grads)
    else:
        grads = long_attention(lax.all_gather(payload, "ctx", axis=0, tiled=True), positions)
        own_grads = lax.dynamic_slice_in_dim(grads, ctx_rank * rows, rows, 1)
        fired, wanted = (
            lax.all_to_all(array.reshape(rows, ctx, features), "ctx", 1, 0).reshape(-1, features)
            for array in (spikes, upstream)
        )
        in_grad = jnp.stack([dot(fired, grads[part], TN) for part in range(3)])
        out_grad = dot(wanted, grads[3], TN)

    own, far, near = spread(fsdp_rank, own_grads, win, out_weight, tokens, gain, inv, factor)
    near = swap(near, "fsdp", 1)
    far = far + near[0]
    own = own + near[1]
    lines = slice(rows, rows + SUM_ROWS)
    line = own[lines] + swap(far[lines], "fsdp", 2)
    landed = swap(jnp.concatenate([far[:rows], far[rows + SUM_ROWS :]]).astype(BF16), "fsdp", 2)
    gain_grad = line[1]
    if short:
        for mask in (1, 2, 4):
            gain_grad = gain_grad + swap(gain_grad, "ctx", mask)
            if mask == 2:
                landed = after(landed, gain_grad)
        landed = after(landed, in_grad, out_grad)
    else:
        gain_grad = lax.psum(gain_grad, "ctx")

    grad_spikes = own[:rows] + landed[:rows].astype(F32)
    token_grad = base + (rise * grad_spikes - fall * line[0, :rows][:, None])
    projected = own[rows + SUM_ROWS :] + landed[rows:].astype(F32)
    block_out = (token_share + projected).astype(BF16)
    return (block_out, token_grad, gain_grad, jnp.transpose(in_grad, (1, 0, 2)), out_grad)


def solution(mesh):
    placed = (
        P("ctx", None),
        P(),
        P(None, "ctx", None),
        P(),
        P(None, None, "fsdp"),
        P("fsdp", None),
        P("ctx", None),
    )
    return jax.shard_map(
        body,
        mesh=mesh,
        in_specs=placed,
        out_specs=(
            P("ctx", "fsdp"),
            P("ctx", "fsdp"),
            P("fsdp"),
            P("ctx", None, "fsdp"),
            P("ctx", "fsdp"),
        ),
        check_vma=False,
    )
```

```python
import functools

import jax
import jax.numpy as jnp
from jax import lax
from jax.experimental import pallas as pl
from jax.experimental.pallas import tpu as pltpu
from jax.sharding import PartitionSpec as P

HEAD_DIM = 128
SOFT_CAP = 30.0
LEAK_RATE = 0.5
THRESHOLD = 1.0
SURRO4_SLOPE = 4.0
EPSILON = 1e-05
SUM_ROWS = 8
LOG2_E = 1.4426950408889634
F32 = jnp.float32
BF16 = jnp.bfloat16


def dot(a, b, dims):
    return lax.dot_general(a, b, (dims, ((), ())), preferred_element_type=F32)


NN = ((1,), (0,))
NT = ((1,), (1,))
TN = ((0,), (0,))


def params(mebibytes=50):
    return pltpu.CompilerParams(vmem_limit_bytes=mebibytes << 20)


def project_kernel(
    at_ref, tok_hbm, pulse_hbm, gain_hbm, win_hbm, up_hbm, wout_hbm, pay_ref, spikes_ref, inv_ref, send_ref,
    tok_ref, pulse_ref, gain_ref, win_ref, up_ref, wout_ref, acc_ref, sems, block_sems,
):
    model = tok_ref.shape[1]
    local = wout_ref.shape[0]
    blocks = block_sems.shape[0]
    width = model // blocks
    ends = [(tok_hbm, tok_ref), (gain_hbm, gain_ref), (up_hbm, up_ref), (wout_hbm, wout_ref)]
    whole = [pltpu.make_async_copy(*pair, sems.at[k]) for k, pair in enumerate(ends)]
    pairs = []
    for k in range(blocks):
        here = pl.ds(k * width, width)
        pulse = (pulse_hbm.at[:, :, here], pulse_ref.at[:, :, here])
        weight = (win_hbm.at[:, here, :], win_ref.at[:, here, :])
        pairs.append(
            [
                pltpu.make_async_copy(*pair, block_sems.at[k, n])
                for n, pair in enumerate((pulse, weight))
            ]
        )
    for copy in [*whole[:2], *(copy for pair in pairs for copy in pair), *whole[2:]]:
        copy.start()
    whole[0].wait()
    values = tok_ref[...].astype(F32)
    inv = lax.rsqrt(jnp.mean(values * values, axis=-1, keepdims=True) + EPSILON)
    inv_ref[...] = inv
    whole[1].wait()
    for k, pair in enumerate(pairs):
        here = slice(k * width, (k + 1) * width)
        pair[0].wait()
        current = tok_ref[:, here].astype(F32) * inv * gain_ref[:, here]
        first = pulse_ref[0, :, here].astype(F32)
        second = pulse_ref[1, :, here].astype(F32)
        later = LEAK_RATE * current * (1.0 - first) + current
        spikes = ((first * current + second * later) * 0.5).astype(BF16)
        spikes_ref[:, here] = spikes
        pair[1].wait()
        for part in range(3):
            columns = slice(part * local, (part + 1) * local)
            share = dot(spikes, win_ref[part, here, :], NN)
            acc_ref[:, columns] = share if k == 0 else acc_ref[:, columns] + share
    pay_ref[:, : 3 * local] = acc_ref[...].astype(BF16)
    for copy in whole[2:]:
        copy.wait()
    pay_ref[:, 3 * local :] = dot(up_ref[...], wout_ref[...], NT).astype(BF16)
    ranks, quarter, both = send_ref.shape
    features = both // 2
    mine = pl.ds(pl.multiple_of(at_ref[0] * quarter, quarter), quarter)
    for rank in range(ranks):
        here = slice(rank * features, (rank + 1) * features)
        send_ref[rank, :, :features] = spikes_ref[mine, here]
        send_ref[rank, :, features:] = up_ref[mine, here]


def project(fsdp_rank, ctx, tokens, pulse, gain, win, upstream, wout):
    rows, model = tokens.shape
    local = wout.shape[0]
    blocks = 4
    arrays = (tokens, pulse, gain, win, upstream, wout)
    in_vmem = pl.BlockSpec(memory_space=pltpu.VMEM)
    return pl.pallas_call(
        project_kernel,
        in_specs=[pl.BlockSpec(memory_space=pltpu.SMEM)]
        + [pl.BlockSpec(memory_space=pltpu.HBM)] * 6,
        out_specs=[in_vmem] * 4,
        out_shape=[
            jax.ShapeDtypeStruct((rows, 4 * local), BF16),
            jax.ShapeDtypeStruct((rows, model), BF16),
            jax.ShapeDtypeStruct((rows, 1), F32),
            jax.ShapeDtypeStruct((ctx, rows // 4, 2 * (model // ctx)), BF16),
        ],
        scratch_shapes=[pltpu.VMEM(array.shape, array.dtype) for array in arrays]
        + [
            pltpu.VMEM((rows, 3 * local), F32),
            pltpu.SemaphoreType.DMA((4,)),
            pltpu.SemaphoreType.DMA((blocks, 2)),
        ],
        compiler_params=params(24),
        name="project",
    )(
        fsdp_rank[None],
        *(pltpu.with_memory_space_constraint(array, pltpu.HBM) for array in arrays),
    )


def factor_kernel(
    at_ref, tok_ref, pulse_ref, gain_ref, inv_ref, up_ref, factor_ref, rise_ref, fall_ref, base_ref, own_ref
):
    model = tok_ref.shape[1]
    width = own_ref.shape[1]
    inv, gain = inv_ref[...], gain_ref[...]
    current = tok_ref[...].astype(F32) * inv * gain
    first = pulse_ref[0].astype(F32)
    second = pulse_ref[1].astype(F32)
    later = LEAK_RATE * current * (1.0 - first) + current

    def slope(fired, membrane):
        level = jax.nn.sigmoid(SURRO4_SLOPE * (membrane - THRESHOLD))
        return fired + membrane * SURRO4_SLOPE * level * (1.0 - level)

    carried = 1.0 + LEAK_RATE * (1.0 - first)
    factor_ref[...] = 0.5 * (slope(first, current) + slope(second, later) * carried)
    here = pl.ds(pl.multiple_of(at_ref[0] * width, width), width)
    own = tok_ref[:, here].astype(F32)
    own_ref[...] = own
    base_ref[...] = up_ref[:, here].astype(F32)
    rise_ref[...] = factor_ref[:, here] * gain_ref[:, here] * inv
    fall_ref[...] = own * inv * (inv / model)


def factors(fsdp_rank, tokens, pulse, gain, inv, upstream, share):
    rows, model = tokens.shape
    in_vmem = pl.BlockSpec(memory_space=pltpu.VMEM)
    return pl.pallas_call(
        factor_kernel,
        in_specs=[pl.BlockSpec(memory_space=pltpu.SMEM)] + [in_vmem] * 5,
        out_specs=[in_vmem] * 5,
        out_shape=[jax.ShapeDtypeStruct((rows, model), F32)]
        + [jax.ShapeDtypeStruct((rows, share), F32)] * 4,
        compiler_params=params(24),
        name="factors",
    )(fsdp_rank[None], tokens, pulse, gain, inv, upstream)


def after(value, *others):
    return lax.optimization_barrier((value, others))[0]


def attend(query, keys, values, grad, allowed):
    scale = HEAD_DIM**-0.5
    squashed = jnp.tanh(dot(query, keys, NT) * (scale / SOFT_CAP))
    exponent = jnp.where(allowed, jnp.exp2((SOFT_CAP * LOG2_E) * squashed), 0.0)
    prob = exponent * (1.0 / jnp.sum(exponent, axis=-1, keepdims=True))
    low = prob.astype(BF16)
    grad_prob = dot(grad, values, NT)
    delta = jnp.sum(prob * grad_prob, axis=-1, keepdims=True)
    score_grad = (prob * (grad_prob - delta) * ((1.0 - squashed * squashed) * scale)).astype(BF16)
    attended = dot(low, values, NN).astype(BF16)
    grad_query = dot(score_grad, keys, NN).astype(BF16)
    return attended, grad_query, dot(score_grad, query, TN), dot(low, grad, TN)


def attention_kernel(*refs):
    *piece_refs, prow_ref, pcol_ref, out_ref, all_ref, dk_ref, dv_ref = refs
    rows = piece_refs[0].shape[0]
    length, width = all_ref.shape
    local = width // 4
    block = length // 2
    for j, piece in enumerate(piece_refs):
        all_ref[j * rows : (j + 1) * rows, :] = piece[...]
    dk_ref[...] = jnp.zeros_like(dk_ref)
    dv_ref[...] = jnp.zeros_like(dv_ref)

    def visit(step, carry):
        at = pl.ds(pl.multiple_of(step * block, block), block)
        allowed = prow_ref[...] <= pcol_ref[at, :]
        for low in range(0, local, HEAD_DIM):
            query, keys, values, grad = (
                slice(part * local + low, part * local + low + HEAD_DIM) for part in range(4)
            )
            here = slice(low, low + HEAD_DIM)
            attended, grad_query, key_part, value_part = attend(
                all_ref[at, query], all_ref[:, keys], all_ref[:, values], all_ref[at, grad], allowed
            )
            out_ref[3, at, here] = attended
            out_ref[0, at, here] = grad_query
            dk_ref[:, here] += key_part
            dv_ref[:, here] += value_part
        return carry

    lax.fori_loop(0, length // block, visit, 0)
    out_ref[1] = dk_ref[...].astype(BF16)
    out_ref[2] = dv_ref[...].astype(BF16)


def attention(pieces, positions):
    rows, width = pieces[0].shape
    length, local = len(pieces) * rows, width // 4
    in_vmem = pl.BlockSpec(memory_space=pltpu.VMEM)
    return pl.pallas_call(
        attention_kernel,
        in_specs=[in_vmem] * (len(pieces) + 2),
        out_specs=in_vmem,
        out_shape=jax.ShapeDtypeStruct((4, length, local), BF16),
        scratch_shapes=[pltpu.VMEM((length, width), BF16)]
        + [pltpu.VMEM((length, local), F32)] * 2,
        compiler_params=params(36),
        name="attention",
    )(*pieces, positions[None, :], positions[:, None])


def long_kernel(q_ref, k_ref, v_ref, do_ref, prow_ref, pcol_ref, out_ref, dk_ref, dv_ref):
    step = pl.program_id(1)
    block = q_ref.shape[0]

    @pl.when(step == 0)
    def _():
        dk_ref[...] = jnp.zeros_like(dk_ref)
        dv_ref[...] = jnp.zeros_like(dv_ref)

    attended, grad_query, key_part, value_part = attend(
        q_ref[...], k_ref[...], v_ref[...], do_ref[...], prow_ref[...] <= pcol_ref[...]
    )
    at = pl.ds(pl.multiple_of(step * block, block), block)
    out_ref[3, at, :] = attended
    out_ref[0, at, :] = grad_query
    dk_ref[...] += key_part
    dv_ref[...] += value_part

    @pl.when(step == pl.num_programs(1) - 1)
    def _():
        out_ref[1] = dk_ref[...].astype(BF16)
        out_ref[2] = dv_ref[...].astype(BF16)


def long_attention(gathered, positions):
    length, width = gathered.shape
    heads = width // (4 * HEAD_DIM)
    block = max(16, (256 * 1024) // length)
    whole = functools.partial(pl.BlockSpec, (length, HEAD_DIM))
    part = functools.partial(pl.BlockSpec, (block, HEAD_DIM))
    return pl.pallas_call(
        long_kernel,
        grid=(heads, length // block),
        in_specs=[
            part(lambda h, i: (i, h)),
            whole(lambda h, i: (0, heads + h)),
            whole(lambda h, i: (0, 2 * heads + h)),
            part(lambda h, i: (i, 3 * heads + h)),
            pl.BlockSpec((1, length), lambda h, i: (0, 0)),
            pl.BlockSpec((block, 1), lambda h, i: (i, 0)),
        ],
        out_specs=pl.BlockSpec((4, length, HEAD_DIM), lambda h, i: (0, 0, h)),
        out_shape=jax.ShapeDtypeStruct((4, length, heads * HEAD_DIM), BF16),
        scratch_shapes=[pltpu.VMEM((length, HEAD_DIM), F32)] * 2,
        compiler_params=params(),
        name="long_attention",
    )(gathered, gathered, gathered, gathered, positions[None, :], positions[:, None])


def spread_kernel(
    at_ref, grad_ref, win_ref, wout_ref, tok_ref, gain_ref, inv_ref, factor_ref,
    own_ref, far_ref, near_ref,
):
    rows = tok_ref.shape[0]
    width = own_ref.shape[1]
    below = rows + SUM_ROWS
    sums = jnp.zeros((rows, 1), F32)
    targets = (own_ref, near_ref.at[1], far_ref, near_ref.at[0])
    for k in range(4):
        here = pl.ds(pl.multiple_of((at_ref[0] ^ k) * width, width), width)
        share = sum(dot(grad_ref[part], win_ref[part, here, :], NT) for part in range(3))
        targets[k][:rows, :] = share
        targets[k][below:, :] = dot(grad_ref[3], wout_ref[:, here], NN)
        weighted = share * factor_ref[:, here] * (tok_ref[:, here].astype(F32) * inv_ref[...])
        targets[k][rows:below, :] = jnp.broadcast_to(
            jnp.sum(weighted, axis=0, keepdims=True), (SUM_ROWS, width)
        )
        sums += jnp.sum(weighted * gain_ref[:, here], axis=1, keepdims=True)
    line = jnp.broadcast_to(sums, (rows, rows)).T[:1, :]
    for target in targets:
        target[rows : rows + 1, :rows] = line


def spread(fsdp_rank, own_grads, win, wout, tokens, gain, inv, factor):
    rows, model = tokens.shape
    width = model // 4
    in_vmem = pl.BlockSpec(memory_space=pltpu.VMEM)
    tall = (2 * rows + SUM_ROWS, width)
    return pl.pallas_call(
        spread_kernel,
        in_specs=[pl.BlockSpec(memory_space=pltpu.SMEM)] + [in_vmem] * 7,
        out_specs=[in_vmem] * 3,
        out_shape=[
            jax.ShapeDtypeStruct(tall, F32),
            jax.ShapeDtypeStruct(tall, F32),
            jax.ShapeDtypeStruct((2,) + tall, F32),
        ],
        compiler_params=params(20),
        name="spread",
    )(fsdp_rank[None], own_grads, win, wout, tokens, gain, inv, factor)


def swap(value, axis, mask):
    count = lax.axis_size(axis)
    return lax.ppermute(value, axis, [(i, i ^ mask) for i in range(count)])


def weight_kernel(at_ref, *refs):
    *piece_refs, grad_ref, in_ref, out_ref, both_ref = refs
    ranks, rows, width = piece_refs[0].shape
    features = width // 2
    for k, piece in enumerate(piece_refs):
        for j in range(ranks):
            low = (j * len(piece_refs) + (at_ref[0] ^ k)) * rows
            both_ref[pl.ds(pl.multiple_of(low, rows), rows), :] = piece[at_ref[1] ^ j]
    fired, wanted = both_ref[:, :features], both_ref[:, features:]
    for part in range(3):
        in_ref[part] = dot(fired, grad_ref[part], TN)
    out_ref[...] = dot(wanted, grad_ref[3], TN)


def weight_grads(fsdp_rank, turn, pieces, grads):
    features = pieces[0].shape[2] // 2
    local = grads.shape[2]
    in_vmem = pl.BlockSpec(memory_space=pltpu.VMEM)
    return pl.pallas_call(
        weight_kernel,
        in_specs=[pl.BlockSpec(memory_space=pltpu.SMEM)] + [in_vmem] * (len(pieces) + 1),
        out_specs=[in_vmem, in_vmem],
        out_shape=[
            jax.ShapeDtypeStruct((3, features, local), F32),
            jax.ShapeDtypeStruct((features, local), F32),
        ],
        scratch_shapes=[pltpu.VMEM((grads.shape[1], 2 * features), BF16)],
        compiler_params=params(16),
        name="weight_grads",
    )(jnp.stack([fsdp_rank, turn]), *pieces, grads)


def body(tokens, positions, pulse_indicator, norm_gain, in_weight, out_weight, upstream):
    ctx, fsdp = lax.axis_size("ctx"), lax.axis_size("fsdp")
    ctx_rank, fsdp_rank = lax.axis_index("ctx"), lax.axis_index("fsdp")
    rows, model = tokens.shape
    local = out_weight.shape[0]
    share = model // fsdp
    gain = norm_gain[None, :]
    features = model // ctx
    win = jnp.transpose(in_weight, (1, 0, 2))
    payload, spikes, inv, both = project(
        fsdp_rank, ctx, tokens, pulse_indicator, gain, win, upstream, out_weight
    )
    factor, rise, fall, base, token_share = factors(
        fsdp_rank, tokens, pulse_indicator, gain, inv, upstream, share
    )

    short = ctx == 8 and fsdp == 4
    if short:
        beside = swap(payload, "ctx", 2)
        below = swap(payload, "ctx", 1)
        across = swap(payload, "ctx", 4)
        diagonal = swap(beside, "ctx", 1)
        corner = swap(across, "ctx", 2)
        across_below = swap(across, "ctx", 1)
        blocks = [payload, below, beside, diagonal, across, across_below]
        blocks += [corner, swap(corner, "ctx", 1)]
        placed = jnp.concatenate(
            [lax.dynamic_slice_in_dim(positions, (ctx_rank ^ j) * rows, rows) for j in range(ctx)]
        )
        both = lax.all_to_all(after(both, below), "ctx", 0, 0)
        over = swap(both, "fsdp", 2)
        pieces = [both, swap(both, "fsdp", 1), over, swap(over, "fsdp", 1)]
        grads = attention(blocks, after(placed, over))
        own_grads = grads[:, :rows]
    else:
        grads = long_attention(lax.all_gather(payload, "ctx", axis=0, tiled=True), positions)
        own_grads = lax.dynamic_slice_in_dim(grads, ctx_rank * rows, rows, 1)
        fired, wanted = (
            lax.all_to_all(array.reshape(rows, ctx, features), "ctx", 1, 0).reshape(-1, features)
            for array in (spikes, upstream)
        )
        in_grad = jnp.stack([dot(fired, grads[part], TN) for part in range(3)])
        out_grad = dot(wanted, grads[3], TN)

    own, far, near = spread(fsdp_rank, own_grads, win, out_weight, tokens, gain, inv, factor)
    near = swap(near, "fsdp", 1)
    far = far + near[0]
    own = own + near[1]
    lines = slice(rows, rows + SUM_ROWS)
    line = own[lines] + swap(far[lines], "fsdp", 2)
    landed = swap(jnp.concatenate([far[:rows], far[rows + SUM_ROWS :]]).astype(BF16), "fsdp", 2)
    gain_grad = line[1]
    if short:
        corner_pairs = [
            (c * fsdp + f, (c ^ 1) * fsdp + (f ^ 2)) for c in range(ctx) for f in range(fsdp)
        ]
        aside = swap(own[rows + 1], "ctx", 1)
        aside = aside + lax.ppermute(far[rows + 1], ("ctx", "fsdp"), corner_pairs)
        gain_grad = gain_grad + aside
        in_grad, out_grad = weight_grads(after(fsdp_rank, gain_grad), ctx_rank, pieces, grads)
        second, third, fourth = (swap(gain_grad, "ctx", mask) for mask in (2, 4, 6))
    else:
        gain_grad = lax.psum(gain_grad, "ctx")

    grad_spikes = own[:rows] + landed[:rows].astype(F32)
    token_grad = base + (rise * grad_spikes - fall * line[0, :rows][:, None])
    projected = own[rows + SUM_ROWS :] + landed[rows:].astype(F32)
    block_out = (token_share + projected).astype(BF16)
    if short:
        third = after(third, token_grad, block_out)
        gain_grad = (gain_grad + second) + (third + fourth)
    return (block_out, token_grad, gain_grad, jnp.transpose(in_grad, (1, 0, 2)), out_grad)


def solution(mesh):
    placed = (
        P("ctx", None),
        P(),
        P(None, "ctx", None),
        P(),
        P(None, None, "fsdp"),
        P("fsdp", None),
        P("ctx", None),
    )
    return jax.shard_map(
        body,
        mesh=mesh,
        in_specs=placed,
        out_specs=(
            P("ctx", "fsdp"),
            P("ctx", "fsdp"),
            P("fsdp"),
            P("ctx", None, "fsdp"),
            P("ctx", "fsdp"),
        ),
        check_vma=False,
    )
```

```python
import functools

import jax
import jax.numpy as jnp
from jax import lax
from jax.experimental import pallas as pl
from jax.experimental.pallas import tpu as pltpu
from jax.sharding import PartitionSpec as P

HEAD_DIM = 128
SOFT_CAP = 30.0
LEAK_RATE = 0.5
THRESHOLD = 1.0
SURRO4_SLOPE = 4.0
EPSILON = 1e-05
SUM_ROWS = 8
LOG2_E = 1.4426950408889634
F32 = jnp.float32
BF16 = jnp.bfloat16


def dot(a, b, dims):
    return lax.dot_general(a, b, (dims, ((), ())), preferred_element_type=F32)


NN = ((1,), (0,))
NT = ((1,), (1,))
TN = ((0,), (0,))


def params(mebibytes=50):
    return pltpu.CompilerParams(vmem_limit_bytes=mebibytes << 20)


def project_kernel(
    at_ref, tok_hbm, pulse_hbm, gain_hbm, win_hbm, up_hbm, wout_hbm, pay_ref, spikes_ref, inv_ref, send_hbm,
    tok_ref, pulse_ref, gain_ref, win_ref, up_ref, wout_ref, acc_ref, ready_ref, sems, block_sems,
):
    model = tok_ref.shape[1]
    local = wout_ref.shape[0]
    blocks = block_sems.shape[0]
    width = model // blocks
    ends = [(tok_hbm, tok_ref), (gain_hbm, gain_ref), (up_hbm, up_ref), (wout_hbm, wout_ref)]
    whole = [pltpu.make_async_copy(*pair, sems.at[k]) for k, pair in enumerate(ends)]
    pairs = []
    for k in range(blocks):
        here = pl.ds(k * width, width)
        pulse = (pulse_hbm.at[:, :, here], pulse_ref.at[:, :, here])
        weight = (win_hbm.at[:, here, :], win_ref.at[:, here, :])
        pairs.append(
            [
                pltpu.make_async_copy(*pair, block_sems.at[k, n])
                for n, pair in enumerate((pulse, weight))
            ]
        )
    for copy in [*whole[:2], *(copy for pair in pairs for copy in pair), *whole[2:]]:
        copy.start()
    whole[0].wait()
    values = tok_ref[...].astype(F32)
    inv = lax.rsqrt(jnp.mean(values * values, axis=-1, keepdims=True) + EPSILON)
    inv_ref[...] = inv
    whole[1].wait()
    for k, pair in enumerate(pairs):
        here = slice(k * width, (k + 1) * width)
        pair[0].wait()
        current = tok_ref[:, here].astype(F32) * inv * gain_ref[:, here]
        first = pulse_ref[0, :, here].astype(F32)
        second = pulse_ref[1, :, here].astype(F32)
        later = LEAK_RATE * current * (1.0 - first) + current
        spikes = ((first * current + second * later) * 0.5).astype(BF16)
        spikes_ref[:, here] = spikes
        pair[1].wait()
        for part in range(3):
            columns = slice(part * local, (part + 1) * local)
            share = dot(spikes, win_ref[part, here, :], NN)
            acc_ref[:, columns] = share if k == 0 else acc_ref[:, columns] + share
    pay_ref[:, : 3 * local] = acc_ref[...].astype(BF16)
    whole[2].wait()
    ranks, quarter, both = ready_ref.shape
    features = both // 2
    mine = pl.ds(pl.multiple_of(at_ref[0] * quarter, quarter), quarter)
    for rank in range(ranks):
        here = slice(rank * features, (rank + 1) * features)
        ready_ref[rank, :, :features] = spikes_ref[mine, here]
        ready_ref[rank, :, features:] = up_ref[mine, here]
    leave = pltpu.make_async_copy(ready_ref, send_hbm, sems.at[4])
    leave.start()
    whole[3].wait()
    pay_ref[:, 3 * local :] = dot(up_ref[...], wout_ref[...], NT).astype(BF16)
    leave.wait()


def project(fsdp_rank, ctx, tokens, pulse, gain, win, upstream, wout):
    rows, model = tokens.shape
    local = wout.shape[0]
    blocks = 4
    arrays = (tokens, pulse, gain, win, upstream, wout)
    in_vmem = pl.BlockSpec(memory_space=pltpu.VMEM)
    return pl.pallas_call(
        project_kernel,
        in_specs=[pl.BlockSpec(memory_space=pltpu.SMEM)]
        + [pl.BlockSpec(memory_space=pltpu.HBM)] * 6,
        out_specs=[in_vmem] * 3 + [pl.BlockSpec(memory_space=pltpu.HBM)],
        out_shape=[
            jax.ShapeDtypeStruct((rows, 4 * local), BF16),
            jax.ShapeDtypeStruct((rows, model), BF16),
            jax.ShapeDtypeStruct((rows, 1), F32),
            pltpu.HBM((ctx, rows // 4, 2 * (model // ctx)), BF16),
        ],
        scratch_shapes=[pltpu.VMEM(array.shape, array.dtype) for array in arrays]
        + [
            pltpu.VMEM((rows, 3 * local), F32),
            pltpu.VMEM((ctx, rows // 4, 2 * (model // ctx)), BF16),
            pltpu.SemaphoreType.DMA((5,)),
            pltpu.SemaphoreType.DMA((blocks, 2)),
        ],
        compiler_params=params(24),
        name="project",
    )(
        fsdp_rank[None],
        *(pltpu.with_memory_space_constraint(array, pltpu.HBM) for array in arrays),
    )


def factor_kernel(
    at_ref, tok_ref, pulse_ref, gain_ref, inv_ref, up_ref, factor_hbm, rise_hbm, fall_hbm, base_hbm, own_hbm,
    factor_ref, rise_ref, fall_ref, base_ref, own_ref, sems,
):
    model = tok_ref.shape[1]
    width = own_ref.shape[1]
    inv, gain = inv_ref[...], gain_ref[...]
    current = tok_ref[...].astype(F32) * inv * gain
    first = pulse_ref[0].astype(F32)
    second = pulse_ref[1].astype(F32)
    later = LEAK_RATE * current * (1.0 - first) + current

    def slope(fired, membrane):
        level = jax.nn.sigmoid(SURRO4_SLOPE * (membrane - THRESHOLD))
        return fired + membrane * SURRO4_SLOPE * level * (1.0 - level)

    carried = 1.0 + LEAK_RATE * (1.0 - first)
    factor_ref[...] = 0.5 * (slope(first, current) + slope(second, later) * carried)
    here = pl.ds(pl.multiple_of(at_ref[0] * width, width), width)
    own = tok_ref[:, here].astype(F32)
    own_ref[...] = own
    base_ref[...] = up_ref[:, here].astype(F32)
    rise_ref[...] = factor_ref[:, here] * gain_ref[:, here] * inv
    fall_ref[...] = own * inv * (inv / model)
    ends = [
        (factor_ref, factor_hbm), (rise_ref, rise_hbm), (fall_ref, fall_hbm), (base_ref, base_hbm), (own_ref, own_hbm)
    ]
    copies = [pltpu.make_async_copy(*pair, sems.at[k]) for k, pair in enumerate(ends)]
    for copy in copies:
        copy.start()
    for copy in copies:
        copy.wait()


def factors(fsdp_rank, tokens, pulse, gain, inv, upstream, share):
    rows, model = tokens.shape
    in_vmem = pl.BlockSpec(memory_space=pltpu.VMEM)
    return pl.pallas_call(
        factor_kernel,
        in_specs=[pl.BlockSpec(memory_space=pltpu.SMEM)] + [in_vmem] * 5,
        out_specs=[pl.BlockSpec(memory_space=pltpu.HBM)] * 5,
        out_shape=[pltpu.HBM((rows, model), F32)] + [pltpu.HBM((rows, share), F32)] * 4,
        scratch_shapes=[pltpu.VMEM((rows, model), F32)]
        + [pltpu.VMEM((rows, share), F32)] * 4
        + [pltpu.SemaphoreType.DMA((5,))],
        compiler_params=params(24),
        name="factors",
    )(fsdp_rank[None], tokens, pulse, gain, inv, upstream)


def after(value, *others):
    return lax.optimization_barrier((value, others))[0]


def attend(query, keys, values, grad, allowed):
    scale = HEAD_DIM**-0.5
    squashed = jnp.tanh(dot(query, keys, NT) * (scale / SOFT_CAP))
    exponent = jnp.where(allowed, jnp.exp2((SOFT_CAP * LOG2_E) * squashed), 0.0)
    prob = exponent * (1.0 / jnp.sum(exponent, axis=-1, keepdims=True))
    low = prob.astype(BF16)
    grad_prob = dot(grad, values, NT)
    delta = jnp.sum(prob * grad_prob, axis=-1, keepdims=True)
    score_grad = (prob * (grad_prob - delta) * (scale - (scale * squashed) * squashed)).astype(BF16)
    attended = dot(low, values, NN).astype(BF16)
    grad_query = dot(score_grad, keys, NN).astype(BF16)
    return attended, grad_query, dot(score_grad, query, TN), dot(low, grad, TN)


def attention_kernel(*refs):
    *piece_refs, prow_ref, pcol_ref, out_ref, all_ref, dk_ref, dv_ref = refs
    rows = piece_refs[0].shape[0]
    length, width = all_ref.shape
    local = width // 4
    block = length
    for j, piece in enumerate(piece_refs):
        all_ref[j * rows : (j + 1) * rows, :] = piece[...]
    dk_ref[...] = jnp.zeros_like(dk_ref)
    dv_ref[...] = jnp.zeros_like(dv_ref)

    def visit(step, carry):
        at = pl.ds(pl.multiple_of(step * block, block), block)
        allowed = prow_ref[...] <= pcol_ref[at, :]
        for low in range(0, local, HEAD_DIM):
            query, keys, values, grad = (
                slice(part * local + low, part * local + low + HEAD_DIM) for part in range(4)
            )
            here = slice(low, low + HEAD_DIM)
            attended, grad_query, key_part, value_part = attend(
                all_ref[at, query], all_ref[:, keys], all_ref[:, values], all_ref[at, grad], allowed
            )
            out_ref[3, at, here] = attended
            out_ref[0, at, here] = grad_query
            dk_ref[:, here] += key_part
            dv_ref[:, here] += value_part
        return carry

    lax.fori_loop(0, length // block, visit, 0)
    out_ref[1] = dk_ref[...].astype(BF16)
    out_ref[2] = dv_ref[...].astype(BF16)


def attention(pieces, positions):
    rows, width = pieces[0].shape
    length, local = len(pieces) * rows, width // 4
    in_vmem = pl.BlockSpec(memory_space=pltpu.VMEM)
    return pl.pallas_call(
        attention_kernel,
        in_specs=[in_vmem] * (len(pieces) + 2),
        out_specs=in_vmem,
        out_shape=jax.ShapeDtypeStruct((4, length, local), BF16),
        scratch_shapes=[pltpu.VMEM((length, width), BF16)]
        + [pltpu.VMEM((length, local), F32)] * 2,
        compiler_params=params(44),
        name="attention",
    )(*pieces, positions[None, :], positions[:, None])


def long_kernel(q_ref, k_ref, v_ref, do_ref, prow_ref, pcol_ref, out_ref, dk_ref, dv_ref):
    step = pl.program_id(1)
    block = q_ref.shape[0]

    @pl.when(step == 0)
    def _():
        dk_ref[...] = jnp.zeros_like(dk_ref)
        dv_ref[...] = jnp.zeros_like(dv_ref)

    attended, grad_query, key_part, value_part = attend(
        q_ref[...], k_ref[...], v_ref[...], do_ref[...], prow_ref[...] <= pcol_ref[...]
    )
    at = pl.ds(pl.multiple_of(step * block, block), block)
    out_ref[3, at, :] = attended
    out_ref[0, at, :] = grad_query
    dk_ref[...] += key_part
    dv_ref[...] += value_part

    @pl.when(step == pl.num_programs(1) - 1)
    def _():
        out_ref[1] = dk_ref[...].astype(BF16)
        out_ref[2] = dv_ref[...].astype(BF16)


def long_attention(gathered, positions):
    length, width = gathered.shape
    heads = width // (4 * HEAD_DIM)
    block = max(16, (256 * 1024) // length)
    whole = functools.partial(pl.BlockSpec, (length, HEAD_DIM))
    part = functools.partial(pl.BlockSpec, (block, HEAD_DIM))
    return pl.pallas_call(
        long_kernel,
        grid=(heads, length // block),
        in_specs=[
            part(lambda h, i: (i, h)),
            whole(lambda h, i: (0, heads + h)),
            whole(lambda h, i: (0, 2 * heads + h)),
            part(lambda h, i: (i, 3 * heads + h)),
            pl.BlockSpec((1, length), lambda h, i: (0, 0)),
            pl.BlockSpec((block, 1), lambda h, i: (i, 0)),
        ],
        out_specs=pl.BlockSpec((4, length, HEAD_DIM), lambda h, i: (0, 0, h)),
        out_shape=jax.ShapeDtypeStruct((4, length, heads * HEAD_DIM), BF16),
        scratch_shapes=[pltpu.VMEM((length, HEAD_DIM), F32)] * 2,
        compiler_params=params(),
        name="long_attention",
    )(gathered, gathered, gathered, gathered, positions[None, :], positions[:, None])


def spread_kernel(
    at_ref, grad_ref, win_ref, wout_ref, tok_ref, gain_ref, inv_ref, factor_ref,
    own_ref, far_ref, near_ref,
):
    rows = tok_ref.shape[0]
    width = own_ref.shape[1]
    below = rows + SUM_ROWS
    sums = jnp.zeros((rows, 1), F32)
    targets = (own_ref, near_ref.at[1], far_ref, near_ref.at[0])
    for k in range(4):
        here = pl.ds(pl.multiple_of((at_ref[0] ^ k) * width, width), width)
        share = sum(dot(grad_ref[part], win_ref[part, here, :], NT) for part in range(3))
        targets[k][:rows, :] = share
        targets[k][below:, :] = dot(grad_ref[3], wout_ref[:, here], NN)
        weighted = share * factor_ref[:, here] * (tok_ref[:, here].astype(F32) * inv_ref[...])
        targets[k][rows:below, :] = jnp.broadcast_to(
            jnp.sum(weighted, axis=0, keepdims=True), (SUM_ROWS, width)
        )
        sums += jnp.sum(weighted * gain_ref[:, here], axis=1, keepdims=True)
    line = jnp.broadcast_to(sums, (rows, rows)).T[:1, :]
    for target in targets:
        target[rows : rows + 1, :rows] = line


def spread(fsdp_rank, own_grads, win, wout, tokens, gain, inv, factor):
    rows, model = tokens.shape
    width = model // 4
    in_vmem = pl.BlockSpec(memory_space=pltpu.VMEM)
    tall = (2 * rows + SUM_ROWS, width)
    return pl.pallas_call(
        spread_kernel,
        in_specs=[pl.BlockSpec(memory_space=pltpu.SMEM)] + [in_vmem] * 7,
        out_specs=[in_vmem] * 3,
        out_shape=[
            jax.ShapeDtypeStruct(tall, F32),
            jax.ShapeDtypeStruct(tall, F32),
            jax.ShapeDtypeStruct((2,) + tall, F32),
        ],
        compiler_params=params(20),
        name="spread",
    )(fsdp_rank[None], own_grads, win, wout, tokens, gain, inv, factor)


def swap(value, axis, mask):
    count = lax.axis_size(axis)
    return lax.ppermute(value, axis, [(i, i ^ mask) for i in range(count)])


def weight_kernel(at_ref, *refs):
    *piece_refs, grad_ref, in_ref, out_ref, both_ref = refs
    ranks, rows, width = piece_refs[0].shape
    features = width // 2
    for k, piece in enumerate(piece_refs):
        for j in range(ranks):
            low = (j * len(piece_refs) + (at_ref[0] ^ k)) * rows
            both_ref[pl.ds(pl.multiple_of(low, rows), rows), :] = piece[at_ref[1] ^ j]
    fired, wanted = both_ref[:, :features], both_ref[:, features:]
    for part in range(3):
        in_ref[part] = dot(fired, grad_ref[part], TN)
    out_ref[...] = dot(wanted, grad_ref[3], TN)


def weight_grads(fsdp_rank, turn, pieces, grads):
    features = pieces[0].shape[2] // 2
    local = grads.shape[2]
    in_vmem = pl.BlockSpec(memory_space=pltpu.VMEM)
    return pl.pallas_call(
        weight_kernel,
        in_specs=[pl.BlockSpec(memory_space=pltpu.SMEM)] + [in_vmem] * (len(pieces) + 1),
        out_specs=[in_vmem, in_vmem],
        out_shape=[
            jax.ShapeDtypeStruct((3, features, local), F32),
            jax.ShapeDtypeStruct((features, local), F32),
        ],
        scratch_shapes=[pltpu.VMEM((grads.shape[1], 2 * features), BF16)],
        compiler_params=params(16),
        name="weight_grads",
    )(jnp.stack([fsdp_rank, turn]), *pieces, grads)


def body(tokens, positions, pulse_indicator, norm_gain, in_weight, out_weight, upstream):
    ctx, fsdp = lax.axis_size("ctx"), lax.axis_size("fsdp")
    ctx_rank, fsdp_rank = lax.axis_index("ctx"), lax.axis_index("fsdp")
    rows, model = tokens.shape
    local = out_weight.shape[0]
    share = model // fsdp
    gain = norm_gain[None, :]
    features = model // ctx
    win = jnp.transpose(in_weight, (1, 0, 2))
    payload, spikes, inv, both = project(
        fsdp_rank, ctx, tokens, pulse_indicator, gain, win, upstream, out_weight
    )
    factor, rise, fall, base, token_share = factors(
        fsdp_rank, tokens, pulse_indicator, gain, inv, upstream, share
    )

    short = ctx == 8 and fsdp == 4
    if short:
        beside = swap(payload, "ctx", 2)
        below = swap(payload, "ctx", 1)
        across = swap(payload, "ctx", 4)
        diagonal = swap(below, "ctx", 2)
        corner = swap(across, "ctx", 2)
        across_below = swap(across, "ctx", 1)
        blocks = [payload, below, beside, diagonal, across, across_below]
        blocks += [corner, swap(corner, "ctx", 1)]
        placed = jnp.concatenate(
            [lax.dynamic_slice_in_dim(positions, (ctx_rank ^ j) * rows, rows) for j in range(ctx)]
        )
        both = lax.all_to_all(after(both, below), "ctx", 0, 0)
        over = swap(both, "fsdp", 2)
        pieces = [both, swap(both, "fsdp", 1), over, swap(over, "fsdp", 1)]
        grads = attention(blocks, after(placed, over))
        own_grads = grads[:, :rows]
    else:
        grads = long_attention(lax.all_gather(payload, "ctx", axis=0, tiled=True), positions)
        own_grads = lax.dynamic_slice_in_dim(grads, ctx_rank * rows, rows, 1)
        fired, wanted = (
            lax.all_to_all(array.reshape(rows, ctx, features), "ctx", 1, 0).reshape(-1, features)
            for array in (spikes, upstream)
        )
        in_grad = jnp.stack([dot(fired, grads[part], TN) for part in range(3)])
        out_grad = dot(wanted, grads[3], TN)

    own, far, near = spread(fsdp_rank, own_grads, win, out_weight, tokens, gain, inv, factor)
    near = swap(near, "fsdp", 1)
    far = far + near[0]
    own = own + near[1]
    lines = slice(rows, rows + SUM_ROWS)
    line = own[lines] + swap(far[lines], "fsdp", 2)
    landed = swap(jnp.concatenate([far[:rows], far[rows + SUM_ROWS :]]).astype(BF16), "fsdp", 2)
    gain_grad = line[1]
    if short:
        corner_pairs = [
            (c * fsdp + f, (c ^ 1) * fsdp + (f ^ 2)) for c in range(ctx) for f in range(fsdp)
        ]
        aside = swap(own[rows + 1], "ctx", 1)
        aside = aside + lax.ppermute(far[rows + 1], ("ctx", "fsdp"), corner_pairs)
        gain_grad = gain_grad + aside
        in_grad, out_grad = weight_grads(after(fsdp_rank, gain_grad), ctx_rank, pieces, grads)
        second, third, fourth = (swap(gain_grad, "ctx", mask) for mask in (2, 4, 6))
    else:
        gain_grad = lax.psum(gain_grad, "ctx")

    grad_spikes = own[:rows] + landed[:rows].astype(F32)
    token_grad = base + (rise * grad_spikes - fall * line[0, :rows][:, None])
    projected = own[rows + SUM_ROWS :] + landed[rows:].astype(F32)
    block_out = (token_share + projected).astype(BF16)
    if short:
        third = after(third, token_grad, block_out)
        gain_grad = (gain_grad + second) + (third + fourth)
    return (block_out, token_grad, gain_grad, jnp.transpose(in_grad, (1, 0, 2)), out_grad)


def solution(mesh):
    placed = (
        P("ctx", None),
        P(),
        P(None, "ctx", None),
        P(),
        P(None, None, "fsdp"),
        P("fsdp", None),
        P("ctx", None),
    )
    return jax.shard_map(
        body,
        mesh=mesh,
        in_specs=placed,
        out_specs=(
            P("ctx", "fsdp"),
            P("ctx", "fsdp"),
            P("fsdp"),
            P("ctx", None, "fsdp"),
            P("ctx", "fsdp"),
        ),
        check_vma=False,
    )
```

```python
import functools

import jax
import jax.numpy as jnp
from jax import lax
from jax.experimental import pallas as pl
from jax.experimental.pallas import tpu as pltpu
from jax.sharding import PartitionSpec as P

HEAD_DIM = 128
SOFT_CAP = 30.0
LEAK_RATE = 0.5
THRESHOLD = 1.0
SURRO4_SLOPE = 4.0
EPSILON = 1e-05
SUM_ROWS = 8
LOG2_E = 1.4426950408889634
F32 = jnp.float32
BF16 = jnp.bfloat16


def dot(a, b, dims):
    return lax.dot_general(a, b, (dims, ((), ())), preferred_element_type=F32)


NN = ((1,), (0,))
NT = ((1,), (1,))
TN = ((0,), (0,))


def params(mebibytes=50):
    return pltpu.CompilerParams(vmem_limit_bytes=mebibytes << 20)


def project_kernel(
    at_ref, tok_hbm, pulse_hbm, gain_hbm, win_hbm, up_hbm, wout_hbm, pay_ref, spikes_ref, inv_ref, send_hbm,
    tok_ref, pulse_ref, gain_ref, win_ref, up_ref, wout_ref, acc_ref, ready_ref, sems, block_sems,
):
    model = tok_ref.shape[1]
    local = wout_ref.shape[0]
    blocks = block_sems.shape[0]
    width = model // blocks
    ends = [(tok_hbm, tok_ref), (gain_hbm, gain_ref), (up_hbm, up_ref), (wout_hbm, wout_ref)]
    whole = [pltpu.make_async_copy(*pair, sems.at[k]) for k, pair in enumerate(ends)]
    pairs = []
    for k in range(blocks):
        here = pl.ds(k * width, width)
        pulse = (pulse_hbm.at[:, :, here], pulse_ref.at[:, :, here])
        weight = (win_hbm.at[:, here, :], win_ref.at[:, here, :])
        pairs.append(
            [
                pltpu.make_async_copy(*pair, block_sems.at[k, n])
                for n, pair in enumerate((pulse, weight))
            ]
        )
    for copy in [*whole[:2], *(copy for pair in pairs for copy in pair), *whole[2:]]:
        copy.start()
    whole[0].wait()
    values = tok_ref[...].astype(F32)
    inv = lax.rsqrt(jnp.mean(values * values, axis=-1, keepdims=True) + EPSILON)
    inv_ref[...] = inv
    whole[1].wait()
    for k, pair in enumerate(pairs):
        here = slice(k * width, (k + 1) * width)
        pair[0].wait()
        current = tok_ref[:, here].astype(F32) * inv * gain_ref[:, here]
        first = pulse_ref[0, :, here].astype(F32)
        second = pulse_ref[1, :, here].astype(F32)
        later = LEAK_RATE * current * (1.0 - first) + current
        spikes = ((first * current + second * later) * 0.5).astype(BF16)
        spikes_ref[:, here] = spikes
        pair[1].wait()
        for part in range(3):
            columns = slice(part * local, (part + 1) * local)
            share = dot(spikes, win_ref[part, here, :], NN)
            acc_ref[:, columns] = share if k == 0 else acc_ref[:, columns] + share
    pay_ref[:, : 3 * local] = acc_ref[...].astype(BF16)
    whole[2].wait()
    ranks, quarter, both = ready_ref.shape
    features = both // 2
    mine = pl.ds(pl.multiple_of(at_ref[0] * quarter, quarter), quarter)
    for rank in range(ranks):
        here = slice(rank * features, (rank + 1) * features)
        ready_ref[rank, :, :features] = spikes_ref[mine, here]
        ready_ref[rank, :, features:] = up_ref[mine, here]
    leave = pltpu.make_async_copy(ready_ref, send_hbm, sems.at[4])
    leave.start()
    whole[3].wait()
    pay_ref[:, 3 * local :] = dot(up_ref[...], wout_ref[...], NT).astype(BF16)
    leave.wait()


def project(fsdp_rank, ctx, tokens, pulse, gain, win, upstream, wout):
    rows, model = tokens.shape
    local = wout.shape[0]
    blocks = 4
    arrays = (tokens, pulse, gain, win, upstream, wout)
    in_vmem = pl.BlockSpec(memory_space=pltpu.VMEM)
    return pl.pallas_call(
        project_kernel,
        in_specs=[pl.BlockSpec(memory_space=pltpu.SMEM)]
        + [pl.BlockSpec(memory_space=pltpu.HBM)] * 6,
        out_specs=[in_vmem] * 3 + [pl.BlockSpec(memory_space=pltpu.HBM)],
        out_shape=[
            jax.ShapeDtypeStruct((rows, 4 * local), BF16),
            jax.ShapeDtypeStruct((rows, model), BF16),
            jax.ShapeDtypeStruct((rows, 1), F32),
            pltpu.HBM((ctx, rows // 4, 2 * (model // ctx)), BF16),
        ],
        scratch_shapes=[pltpu.VMEM(array.shape, array.dtype) for array in arrays]
        + [
            pltpu.VMEM((rows, 3 * local), F32),
            pltpu.VMEM((ctx, rows // 4, 2 * (model // ctx)), BF16),
            pltpu.SemaphoreType.DMA((5,)),
            pltpu.SemaphoreType.DMA((blocks, 2)),
        ],
        compiler_params=params(24),
        name="project",
    )(
        fsdp_rank[None],
        *(pltpu.with_memory_space_constraint(array, pltpu.HBM) for array in arrays),
    )


def factor_kernel(
    at_ref, tok_ref, pulse_ref, gain_ref, inv_ref, up_ref, factor_hbm, rise_hbm, fall_hbm, base_hbm, own_hbm,
    factor_ref, rise_ref, fall_ref, base_ref, own_ref, sems,
):
    model = tok_ref.shape[1]
    width = own_ref.shape[1]
    inv, gain = inv_ref[...], gain_ref[...]
    current = tok_ref[...].astype(F32) * inv * gain
    first = pulse_ref[0].astype(F32)
    second = pulse_ref[1].astype(F32)
    later = LEAK_RATE * current * (1.0 - first) + current

    def slope(fired, membrane):
        level = jax.nn.sigmoid(SURRO4_SLOPE * (membrane - THRESHOLD))
        return fired + membrane * SURRO4_SLOPE * level * (1.0 - level)

    carried = 1.0 + LEAK_RATE * (1.0 - first)
    factor_ref[...] = 0.5 * (slope(first, current) + slope(second, later) * carried)
    here = pl.ds(pl.multiple_of(at_ref[0] * width, width), width)
    own = tok_ref[:, here].astype(F32)
    own_ref[...] = own
    base_ref[...] = up_ref[:, here].astype(F32)
    rise_ref[...] = factor_ref[:, here] * gain_ref[:, here] * inv
    fall_ref[...] = own * inv * (inv / model)
    ends = [
        (factor_ref, factor_hbm), (rise_ref, rise_hbm), (fall_ref, fall_hbm), (base_ref, base_hbm), (own_ref, own_hbm)
    ]
    copies = [pltpu.make_async_copy(*pair, sems.at[k]) for k, pair in enumerate(ends)]
    for copy in copies:
        copy.start()
    for copy in copies:
        copy.wait()


def factors(fsdp_rank, tokens, pulse, gain, inv, upstream, share):
    rows, model = tokens.shape
    in_vmem = pl.BlockSpec(memory_space=pltpu.VMEM)
    return pl.pallas_call(
        factor_kernel,
        in_specs=[pl.BlockSpec(memory_space=pltpu.SMEM)] + [in_vmem] * 5,
        out_specs=[pl.BlockSpec(memory_space=pltpu.HBM)] * 5,
        out_shape=[pltpu.HBM((rows, model), F32)] + [pltpu.HBM((rows, share), F32)] * 4,
        scratch_shapes=[pltpu.VMEM((rows, model), F32)]
        + [pltpu.VMEM((rows, share), F32)] * 4
        + [pltpu.SemaphoreType.DMA((5,))],
        compiler_params=params(24),
        name="factors",
    )(fsdp_rank[None], tokens, pulse, gain, inv, upstream)


def after(value, *others):
    return lax.optimization_barrier((value, others))[0]


def attend(query, keys, values, grad, allowed):
    scale = HEAD_DIM**-0.5
    squashed = jnp.tanh(dot(query, keys, NT) * (scale / SOFT_CAP))
    exponent = jnp.where(allowed, jnp.exp2((SOFT_CAP * LOG2_E) * squashed), 0.0)
    prob = exponent * (1.0 / jnp.sum(exponent, axis=-1, keepdims=True))
    low = prob.astype(BF16)
    grad_prob = dot(grad, values, NT)
    delta = jnp.sum(prob * grad_prob, axis=-1, keepdims=True)
    score_grad = (prob * (grad_prob - delta) * (scale - (scale * squashed) * squashed)).astype(BF16)
    attended = dot(low, values, NN).astype(BF16)
    grad_query = dot(score_grad, keys, NN).astype(BF16)
    return attended, grad_query, dot(score_grad, query, TN), dot(low, grad, TN)


def attention_kernel(*refs):
    *piece_refs, prow_ref, pcol_ref, out_ref, all_ref, sems = refs
    rows = piece_refs[0].shape[0]
    local = all_ref.shape[1] // 4
    copies = [
        pltpu.make_async_copy(piece, all_ref.at[pl.ds(j * rows, rows), :], sems.at[j])
        for j, piece in enumerate(piece_refs)
    ]
    for copy in copies:
        copy.start()
    for copy in copies:
        copy.wait()
    allowed = prow_ref[...] <= pcol_ref[...]
    for low in range(0, local, HEAD_DIM):
        query, keys, values, grad = (
            all_ref[:, part * local + low : part * local + low + HEAD_DIM] for part in range(4)
        )
        attended, grad_query, grad_keys, grad_values = attend(query, keys, values, grad, allowed)
        here = slice(low, low + HEAD_DIM)
        out_ref[0, :, here] = grad_query
        out_ref[1, :, here] = grad_keys.astype(BF16)
        out_ref[2, :, here] = grad_values.astype(BF16)
        out_ref[3, :, here] = attended


def attention(pieces, positions):
    rows, width = pieces[0].shape
    length, local = len(pieces) * rows, width // 4
    in_vmem = pl.BlockSpec(memory_space=pltpu.VMEM)
    return pl.pallas_call(
        attention_kernel,
        in_specs=[pl.BlockSpec(memory_space=pl.ANY)] * len(pieces) + [in_vmem] * 2,
        out_specs=in_vmem,
        out_shape=jax.ShapeDtypeStruct((4, length, local), BF16),
        scratch_shapes=[pltpu.VMEM((length, width), BF16), pltpu.SemaphoreType.DMA((len(pieces),))],
        compiler_params=params(44),
        name="attention",
    )(*pieces, positions[None, :], positions[:, None])


def long_kernel(q_ref, k_ref, v_ref, do_ref, prow_ref, pcol_ref, out_ref, dk_ref, dv_ref):
    step = pl.program_id(1)
    block = q_ref.shape[0]

    @pl.when(step == 0)
    def _():
        dk_ref[...] = jnp.zeros_like(dk_ref)
        dv_ref[...] = jnp.zeros_like(dv_ref)

    attended, grad_query, key_part, value_part = attend(
        q_ref[...], k_ref[...], v_ref[...], do_ref[...], prow_ref[...] <= pcol_ref[...]
    )
    at = pl.ds(pl.multiple_of(step * block, block), block)
    out_ref[3, at, :] = attended
    out_ref[0, at, :] = grad_query
    dk_ref[...] += key_part
    dv_ref[...] += value_part

    @pl.when(step == pl.num_programs(1) - 1)
    def _():
        out_ref[1] = dk_ref[...].astype(BF16)
        out_ref[2] = dv_ref[...].astype(BF16)


def long_attention(gathered, positions):
    length, width = gathered.shape
    heads = width // (4 * HEAD_DIM)
    block = max(16, (256 * 1024) // length)
    whole = functools.partial(pl.BlockSpec, (length, HEAD_DIM))
    part = functools.partial(pl.BlockSpec, (block, HEAD_DIM))
    return pl.pallas_call(
        long_kernel,
        grid=(heads, length // block),
        in_specs=[
            part(lambda h, i: (i, h)),
            whole(lambda h, i: (0, heads + h)),
            whole(lambda h, i: (0, 2 * heads + h)),
            part(lambda h, i: (i, 3 * heads + h)),
            pl.BlockSpec((1, length), lambda h, i: (0, 0)),
            pl.BlockSpec((block, 1), lambda h, i: (i, 0)),
        ],
        out_specs=pl.BlockSpec((4, length, HEAD_DIM), lambda h, i: (0, 0, h)),
        out_shape=jax.ShapeDtypeStruct((4, length, heads * HEAD_DIM), BF16),
        scratch_shapes=[pltpu.VMEM((length, HEAD_DIM), F32)] * 2,
        compiler_params=params(),
        name="long_attention",
    )(gathered, gathered, gathered, gathered, positions[None, :], positions[:, None])


def spread_kernel(
    at_ref, grad_ref, win_ref, wout_ref, tok_ref, gain_ref, inv_ref, factor_ref,
    own_ref, far_ref, near_ref,
):
    rows = tok_ref.shape[0]
    width = own_ref.shape[1]
    below = rows + SUM_ROWS
    sums = jnp.zeros((rows, 1), F32)
    targets = (own_ref, near_ref.at[1], far_ref, near_ref.at[0])
    for k in range(4):
        here = pl.ds(pl.multiple_of((at_ref[0] ^ k) * width, width), width)
        share = sum(dot(grad_ref[part], win_ref[part, here, :], NT) for part in range(3))
        targets[k][:rows, :] = share
        targets[k][below:, :] = dot(grad_ref[3], wout_ref[:, here], NN)
        weighted = share * factor_ref[:, here] * (tok_ref[:, here].astype(F32) * inv_ref[...])
        targets[k][rows:below, :] = jnp.broadcast_to(
            jnp.sum(weighted, axis=0, keepdims=True), (SUM_ROWS, width)
        )
        sums += jnp.sum(weighted * gain_ref[:, here], axis=1, keepdims=True)
    line = jnp.broadcast_to(sums, (rows, rows)).T[:1, :]
    for target in targets:
        target[rows : rows + 1, :rows] = line


def spread(fsdp_rank, own_grads, win, wout, tokens, gain, inv, factor):
    rows, model = tokens.shape
    width = model // 4
    in_vmem = pl.BlockSpec(memory_space=pltpu.VMEM)
    tall = (2 * rows + SUM_ROWS, width)
    return pl.pallas_call(
        spread_kernel,
        in_specs=[pl.BlockSpec(memory_space=pltpu.SMEM)] + [in_vmem] * 7,
        out_specs=[in_vmem] * 3,
        out_shape=[
            jax.ShapeDtypeStruct(tall, F32),
            jax.ShapeDtypeStruct(tall, F32),
            jax.ShapeDtypeStruct((2,) + tall, F32),
        ],
        compiler_params=params(20),
        name="spread",
    )(fsdp_rank[None], own_grads, win, wout, tokens, gain, inv, factor)


def swap(value, axis, mask):
    count = lax.axis_size(axis)
    return lax.ppermute(value, axis, [(i, i ^ mask) for i in range(count)])


def weight_kernel(at_ref, *refs):
    *piece_refs, grad_ref, in_ref, out_ref, both_ref = refs
    ranks, rows, width = piece_refs[0].shape
    features = width // 2
    for k, piece in enumerate(piece_refs):
        for j in range(ranks):
            low = (j * len(piece_refs) + (at_ref[0] ^ k)) * rows
            both_ref[pl.ds(pl.multiple_of(low, rows), rows), :] = piece[at_ref[1] ^ j]
    fired, wanted = both_ref[:, :features], both_ref[:, features:]
    for part in range(3):
        in_ref[part] = dot(fired, grad_ref[part], TN)
    out_ref[...] = dot(wanted, grad_ref[3], TN)


def weight_grads(fsdp_rank, turn, pieces, grads):
    features = pieces[0].shape[2] // 2
    local = grads.shape[2]
    in_vmem = pl.BlockSpec(memory_space=pltpu.VMEM)
    return pl.pallas_call(
        weight_kernel,
        in_specs=[pl.BlockSpec(memory_space=pltpu.SMEM)] + [in_vmem] * (len(pieces) + 1),
        out_specs=[in_vmem, in_vmem],
        out_shape=[
            jax.ShapeDtypeStruct((3, features, local), F32),
            jax.ShapeDtypeStruct((features, local), F32),
        ],
        scratch_shapes=[pltpu.VMEM((grads.shape[1], 2 * features), BF16)],
        compiler_params=params(16),
        name="weight_grads",
    )(jnp.stack([fsdp_rank, turn]), *pieces, grads)


def body(tokens, positions, pulse_indicator, norm_gain, in_weight, out_weight, upstream):
    ctx, fsdp = lax.axis_size("ctx"), lax.axis_size("fsdp")
    ctx_rank, fsdp_rank = lax.axis_index("ctx"), lax.axis_index("fsdp")
    rows, model = tokens.shape
    local = out_weight.shape[0]
    share = model // fsdp
    gain = norm_gain[None, :]
    features = model // ctx
    win = jnp.transpose(in_weight, (1, 0, 2))
    payload, spikes, inv, both = project(
        fsdp_rank, ctx, tokens, pulse_indicator, gain, win, upstream, out_weight
    )
    factor, rise, fall, base, token_share = factors(
        fsdp_rank, tokens, pulse_indicator, gain, inv, upstream, share
    )

    short = ctx == 8 and fsdp == 4
    if short:
        beside = swap(payload, "ctx", 2)
        below = swap(payload, "ctx", 1)
        across = swap(payload, "ctx", 4)
        diagonal = swap(below, "ctx", 2)
        corner = swap(across, "ctx", 2)
        across_below = swap(across, "ctx", 1)
        blocks = [payload, below, beside, diagonal, across, across_below]
        blocks += [corner, swap(corner, "ctx", 1)]
        blocks[1] = pltpu.with_memory_space_constraint(below, pltpu.HBM)
        placed = jnp.concatenate(
            [lax.dynamic_slice_in_dim(positions, (ctx_rank ^ j) * rows, rows) for j in range(ctx)]
        )
        both = lax.all_to_all(after(both, below), "ctx", 0, 0)
        over = swap(both, "fsdp", 2)
        pieces = [both, swap(both, "fsdp", 1), over, swap(over, "fsdp", 1)]
        grads = attention(blocks, after(placed, over))
        own_grads = grads[:, :rows]
    else:
        grads = long_attention(lax.all_gather(payload, "ctx", axis=0, tiled=True), positions)
        own_grads = lax.dynamic_slice_in_dim(grads, ctx_rank * rows, rows, 1)
        fired, wanted = (
            lax.all_to_all(array.reshape(rows, ctx, features), "ctx", 1, 0).reshape(-1, features)
            for array in (spikes, upstream)
        )
        in_grad = jnp.stack([dot(fired, grads[part], TN) for part in range(3)])
        out_grad = dot(wanted, grads[3], TN)

    own, far, near = spread(fsdp_rank, own_grads, win, out_weight, tokens, gain, inv, factor)
    near = swap(near, "fsdp", 1)
    far = far + near[0]
    own = own + near[1]
    lines = slice(rows, rows + SUM_ROWS)
    line = own[lines] + swap(far[lines], "fsdp", 2)
    landed = swap(jnp.concatenate([far[:rows], far[rows + SUM_ROWS :]]).astype(BF16), "fsdp", 2)
    gain_grad = line[1]
    if short:
        corner_pairs = [
            (c * fsdp + f, (c ^ 1) * fsdp + (f ^ 2)) for c in range(ctx) for f in range(fsdp)
        ]
        aside = swap(own[rows + 1], "ctx", 1)
        aside = aside + lax.ppermute(far[rows + 1], ("ctx", "fsdp"), corner_pairs)
        gain_grad = gain_grad + aside
        in_grad, out_grad = weight_grads(after(fsdp_rank, gain_grad), ctx_rank, pieces, grads)
        second, third, fourth = (swap(gain_grad, "ctx", mask) for mask in (2, 4, 6))
    else:
        gain_grad = lax.psum(gain_grad, "ctx")

    grad_spikes = own[:rows] + landed[:rows].astype(F32)
    token_grad = base + (rise * grad_spikes - fall * line[0, :rows][:, None])
    projected = own[rows + SUM_ROWS :] + landed[rows:].astype(F32)
    block_out = (token_share + projected).astype(BF16)
    if short:
        third = after(third, token_grad, block_out)
        gain_grad = (gain_grad + second) + (third + fourth)
    return (block_out, token_grad, gain_grad, jnp.transpose(in_grad, (1, 0, 2)), out_grad)


def solution(mesh):
    placed = (
        P("ctx", None),
        P(),
        P(None, "ctx", None),
        P(),
        P(None, None, "fsdp"),
        P("fsdp", None),
        P("ctx", None),
    )
    return jax.shard_map(
        body,
        mesh=mesh,
        in_specs=placed,
        out_specs=(
            P("ctx", "fsdp"),
            P("ctx", "fsdp"),
            P("fsdp"),
            P("ctx", None, "fsdp"),
            P("ctx", "fsdp"),
        ),
        check_vma=False,
    )
```

```python
import functools

import jax
import jax.numpy as jnp
from jax import lax
from jax.experimental import pallas as pl
from jax.experimental.pallas import tpu as pltpu
from jax.sharding import PartitionSpec as P

HEAD_DIM = 128
SOFT_CAP = 30.0
LEAK_RATE = 0.5
THRESHOLD = 1.0
SURRO4_SLOPE = 4.0
EPSILON = 1e-05
SUM_ROWS = 8
LOG2_E = 1.4426950408889634
F32 = jnp.float32
BF16 = jnp.bfloat16


def dot(a, b, dims):
    return lax.dot_general(a, b, (dims, ((), ())), preferred_element_type=F32)


NN = ((1,), (0,))
NT = ((1,), (1,))
TN = ((0,), (0,))


def params(mebibytes=50):
    return pltpu.CompilerParams(vmem_limit_bytes=mebibytes << 20)


def project_kernel(
    at_ref, tok_hbm, pulse_hbm, gain_hbm, win_hbm, up_hbm, wout_hbm, pay_ref, spikes_ref, inv_ref, send_hbm,
    tok_ref, pulse_ref, gain_ref, win_ref, up_ref, wout_ref, acc_ref, ready_ref, sems, block_sems,
):
    model = tok_ref.shape[1]
    local = wout_ref.shape[0]
    blocks = block_sems.shape[0]
    width = model // blocks
    ends = [(tok_hbm, tok_ref), (gain_hbm, gain_ref), (up_hbm, up_ref), (wout_hbm, wout_ref)]
    whole = [pltpu.make_async_copy(*pair, sems.at[k]) for k, pair in enumerate(ends)]
    pairs = []
    for k in range(blocks):
        here = pl.ds(k * width, width)
        pulse = (pulse_hbm.at[:, :, here], pulse_ref.at[:, :, here])
        weight = (win_hbm.at[:, here, :], win_ref.at[:, here, :])
        pairs.append(
            [
                pltpu.make_async_copy(*pair, block_sems.at[k, n])
                for n, pair in enumerate((pulse, weight))
            ]
        )
    for copy in [*whole[:2], *(copy for pair in pairs for copy in pair), *whole[2:]]:
        copy.start()
    whole[0].wait()
    values = tok_ref[...].astype(F32)
    inv = lax.rsqrt(jnp.mean(values * values, axis=-1, keepdims=True) + EPSILON)
    inv_ref[...] = inv
    whole[1].wait()
    for k, pair in enumerate(pairs):
        here = slice(k * width, (k + 1) * width)
        pair[0].wait()
        current = tok_ref[:, here].astype(F32) * inv * gain_ref[:, here]
        first = pulse_ref[0, :, here].astype(F32)
        second = pulse_ref[1, :, here].astype(F32)
        later = LEAK_RATE * current * (1.0 - first) + current
        spikes = ((first * current + second * later) * 0.5).astype(BF16)
        spikes_ref[:, here] = spikes
        pair[1].wait()
        for part in range(3):
            columns = slice(part * local, (part + 1) * local)
            share = dot(spikes, win_ref[part, here, :], NN)
            acc_ref[:, columns] = share if k == 0 else acc_ref[:, columns] + share
    pay_ref[:, : 3 * local] = acc_ref[...].astype(BF16)
    whole[2].wait()
    ranks, quarter, both = ready_ref.shape
    features = both // 2
    mine = pl.ds(pl.multiple_of(at_ref[0] * quarter, quarter), quarter)
    for rank in range(ranks):
        here = slice(rank * features, (rank + 1) * features)
        ready_ref[rank, :, :features] = spikes_ref[mine, here]
        ready_ref[rank, :, features:] = up_ref[mine, here]
    leave = pltpu.make_async_copy(ready_ref, send_hbm, sems.at[4])
    leave.start()
    whole[3].wait()
    pay_ref[:, 3 * local :] = dot(up_ref[...], wout_ref[...], NT).astype(BF16)
    leave.wait()


def project(fsdp_rank, ctx, tokens, pulse, gain, win, upstream, wout):
    rows, model = tokens.shape
    local = wout.shape[0]
    blocks = 2
    arrays = (tokens, pulse, gain, win, upstream, wout)
    in_vmem = pl.BlockSpec(memory_space=pltpu.VMEM)
    return pl.pallas_call(
        project_kernel,
        in_specs=[pl.BlockSpec(memory_space=pltpu.SMEM)]
        + [pl.BlockSpec(memory_space=pltpu.HBM)] * 6,
        out_specs=[in_vmem] * 3 + [pl.BlockSpec(memory_space=pltpu.HBM)],
        out_shape=[
            jax.ShapeDtypeStruct((rows, 4 * local), BF16),
            jax.ShapeDtypeStruct((rows, model), BF16),
            jax.ShapeDtypeStruct((rows, 1), F32),
            pltpu.HBM((ctx, rows // 4, 2 * (model // ctx)), BF16),
        ],
        scratch_shapes=[pltpu.VMEM(array.shape, array.dtype) for array in arrays]
        + [
            pltpu.VMEM((rows, 3 * local), F32),
            pltpu.VMEM((ctx, rows // 4, 2 * (model // ctx)), BF16),
            pltpu.SemaphoreType.DMA((5,)),
            pltpu.SemaphoreType.DMA((blocks, 2)),
        ],
        compiler_params=params(24),
        name="project",
    )(
        fsdp_rank[None],
        *(pltpu.with_memory_space_constraint(array, pltpu.HBM) for array in arrays),
    )


def factor_kernel(
    at_ref, tok_ref, pulse_ref, gain_ref, inv_ref, up_ref, factor_hbm, rise_hbm, fall_hbm, base_hbm, own_hbm,
    factor_ref, rise_ref, fall_ref, base_ref, own_ref, sems,
):
    model = tok_ref.shape[1]
    width = own_ref.shape[1]
    inv, gain = inv_ref[...], gain_ref[...]
    current = tok_ref[...].astype(F32) * inv * gain
    first = pulse_ref[0].astype(F32)
    second = pulse_ref[1].astype(F32)
    later = LEAK_RATE * current * (1.0 - first) + current

    def slope(fired, membrane):
        level = jax.nn.sigmoid(SURRO4_SLOPE * (membrane - THRESHOLD))
        return fired + membrane * SURRO4_SLOPE * level * (1.0 - level)

    carried = 1.0 + LEAK_RATE * (1.0 - first)
    factor_ref[...] = 0.5 * (slope(first, current) + slope(second, later) * carried)
    here = pl.ds(pl.multiple_of(at_ref[0] * width, width), width)
    own = tok_ref[:, here].astype(F32)
    own_ref[...] = own
    base_ref[...] = up_ref[:, here].astype(F32)
    rise_ref[...] = factor_ref[:, here] * gain_ref[:, here] * inv
    fall_ref[...] = own * inv * (inv / model)
    ends = [
        (factor_ref, factor_hbm), (rise_ref, rise_hbm), (fall_ref, fall_hbm), (base_ref, base_hbm), (own_ref, own_hbm)
    ]
    copies = [pltpu.make_async_copy(*pair, sems.at[k]) for k, pair in enumerate(ends)]
    for copy in copies:
        copy.start()
    for copy in copies:
        copy.wait()


def factors(fsdp_rank, tokens, pulse, gain, inv, upstream, share):
    rows, model = tokens.shape
    in_vmem = pl.BlockSpec(memory_space=pltpu.VMEM)
    return pl.pallas_call(
        factor_kernel,
        in_specs=[pl.BlockSpec(memory_space=pltpu.SMEM)] + [in_vmem] * 5,
        out_specs=[pl.BlockSpec(memory_space=pltpu.HBM)] * 5,
        out_shape=[pltpu.HBM((rows, model), F32)] + [pltpu.HBM((rows, share), F32)] * 4,
        scratch_shapes=[pltpu.VMEM((rows, model), F32)]
        + [pltpu.VMEM((rows, share), F32)] * 4
        + [pltpu.SemaphoreType.DMA((5,))],
        compiler_params=params(24),
        name="factors",
    )(fsdp_rank[None], tokens, pulse, gain, inv, upstream)


def after(value, *others):
    return lax.optimization_barrier((value, others))[0]


def attend(query, keys, values, grad, allowed):
    scale = HEAD_DIM**-0.5
    squashed = jnp.tanh(dot(query, keys, NT) * (scale / SOFT_CAP))
    exponent = jnp.where(allowed, jnp.exp2((SOFT_CAP * LOG2_E) * squashed), 0.0)
    prob = exponent * (1.0 / jnp.sum(exponent, axis=-1, keepdims=True))
    low = prob.astype(BF16)
    grad_prob = dot(grad, values, NT)
    delta = jnp.sum(prob * grad_prob, axis=-1, keepdims=True)
    score_grad = (prob * (grad_prob - delta) * (scale - (scale * squashed) * squashed)).astype(BF16)
    attended = dot(low, values, NN).astype(BF16)
    grad_query = dot(score_grad, keys, NN).astype(BF16)
    return attended, grad_query, dot(score_grad, query, TN), dot(low, grad, TN)


def attention_kernel(*refs):
    *piece_refs, prow_ref, pcol_ref, out_ref, all_ref, sems = refs
    rows = piece_refs[0].shape[0]
    local = all_ref.shape[1] // 4
    copies = [
        pltpu.make_async_copy(piece, all_ref.at[pl.ds(j * rows, rows), :], sems.at[j])
        for j, piece in enumerate(piece_refs)
    ]
    for copy in copies:
        copy.start()
    for copy in copies:
        copy.wait()
    allowed = prow_ref[...] <= pcol_ref[...]
    for low in range(0, local, HEAD_DIM):
        query, keys, values, grad = (
            all_ref[:, part * local + low : part * local + low + HEAD_DIM] for part in range(4)
        )
        attended, grad_query, grad_keys, grad_values = attend(query, keys, values, grad, allowed)
        here = slice(low, low + HEAD_DIM)
        out_ref[0, :, here] = grad_query
        out_ref[1, :, here] = grad_keys.astype(BF16)
        out_ref[2, :, here] = grad_values.astype(BF16)
        out_ref[3, :, here] = attended


def attention(pieces, positions):
    rows, width = pieces[0].shape
    length, local = len(pieces) * rows, width // 4
    in_vmem = pl.BlockSpec(memory_space=pltpu.VMEM)
    return pl.pallas_call(
        attention_kernel,
        in_specs=[pl.BlockSpec(memory_space=pl.ANY)] * len(pieces) + [in_vmem] * 2,
        out_specs=in_vmem,
        out_shape=jax.ShapeDtypeStruct((4, length, local), BF16),
        scratch_shapes=[pltpu.VMEM((length, width), BF16), pltpu.SemaphoreType.DMA((len(pieces),))],
        compiler_params=params(44),
        name="attention",
    )(*pieces, positions[None, :], positions[:, None])


def long_kernel(q_ref, k_ref, v_ref, do_ref, prow_ref, pcol_ref, out_ref, dk_ref, dv_ref):
    step = pl.program_id(1)
    block = q_ref.shape[0]

    @pl.when(step == 0)
    def _():
        dk_ref[...] = jnp.zeros_like(dk_ref)
        dv_ref[...] = jnp.zeros_like(dv_ref)

    attended, grad_query, key_part, value_part = attend(
        q_ref[...], k_ref[...], v_ref[...], do_ref[...], prow_ref[...] <= pcol_ref[...]
    )
    at = pl.ds(pl.multiple_of(step * block, block), block)
    out_ref[3, at, :] = attended
    out_ref[0, at, :] = grad_query
    dk_ref[...] += key_part
    dv_ref[...] += value_part

    @pl.when(step == pl.num_programs(1) - 1)
    def _():
        out_ref[1] = dk_ref[...].astype(BF16)
        out_ref[2] = dv_ref[...].astype(BF16)


def long_attention(gathered, positions):
    length, width = gathered.shape
    heads = width // (4 * HEAD_DIM)
    block = max(16, (256 * 1024) // length)
    whole = functools.partial(pl.BlockSpec, (length, HEAD_DIM))
    part = functools.partial(pl.BlockSpec, (block, HEAD_DIM))
    return pl.pallas_call(
        long_kernel,
        grid=(heads, length // block),
        in_specs=[
            part(lambda h, i: (i, h)),
            whole(lambda h, i: (0, heads + h)),
            whole(lambda h, i: (0, 2 * heads + h)),
            part(lambda h, i: (i, 3 * heads + h)),
            pl.BlockSpec((1, length), lambda h, i: (0, 0)),
            pl.BlockSpec((block, 1), lambda h, i: (i, 0)),
        ],
        out_specs=pl.BlockSpec((4, length, HEAD_DIM), lambda h, i: (0, 0, h)),
        out_shape=jax.ShapeDtypeStruct((4, length, heads * HEAD_DIM), BF16),
        scratch_shapes=[pltpu.VMEM((length, HEAD_DIM), F32)] * 2,
        compiler_params=params(),
        name="long_attention",
    )(gathered, gathered, gathered, gathered, positions[None, :], positions[:, None])


def spread_kernel(
    at_ref, grad_ref, win_ref, wout_ref, tok_ref, gain_ref, inv_ref, factor_ref,
    own_ref, far_ref, near_ref,
):
    rows = tok_ref.shape[0]
    width = own_ref.shape[1]
    below = rows + SUM_ROWS
    sums = jnp.zeros((rows, 1), F32)
    targets = (own_ref, near_ref.at[1], far_ref, near_ref.at[0])
    for k in range(4):
        here = pl.ds(pl.multiple_of((at_ref[0] ^ k) * width, width), width)
        share = sum(dot(grad_ref[part], win_ref[part, here, :], NT) for part in range(3))
        targets[k][:rows, :] = share
        targets[k][below:, :] = dot(grad_ref[3], wout_ref[:, here], NN)
        weighted = share * factor_ref[:, here] * (tok_ref[:, here].astype(F32) * inv_ref[...])
        targets[k][rows:below, :] = jnp.broadcast_to(
            jnp.sum(weighted, axis=0, keepdims=True), (SUM_ROWS, width)
        )
        sums += jnp.sum(weighted * gain_ref[:, here], axis=1, keepdims=True)
    line = jnp.broadcast_to(sums, (rows, rows)).T[:1, :]
    for target in targets:
        target[rows : rows + 1, :rows] = line


def spread(fsdp_rank, own_grads, win, wout, tokens, gain, inv, factor):
    rows, model = tokens.shape
    width = model // 4
    in_vmem = pl.BlockSpec(memory_space=pltpu.VMEM)
    tall = (2 * rows + SUM_ROWS, width)
    return pl.pallas_call(
        spread_kernel,
        in_specs=[pl.BlockSpec(memory_space=pltpu.SMEM)] + [in_vmem] * 7,
        out_specs=[in_vmem] * 3,
        out_shape=[
            jax.ShapeDtypeStruct(tall, F32),
            jax.ShapeDtypeStruct(tall, F32),
            jax.ShapeDtypeStruct((2,) + tall, F32),
        ],
        compiler_params=params(20),
        name="spread",
    )(fsdp_rank[None], own_grads, win, wout, tokens, gain, inv, factor)


def swap(value, axis, mask):
    count = lax.axis_size(axis)
    return lax.ppermute(value, axis, [(i, i ^ mask) for i in range(count)])


def weight_kernel(at_ref, *refs):
    *piece_refs, grad_ref, in_ref, out_ref, both_ref = refs
    ranks, rows, width = piece_refs[0].shape
    features = width // 2
    for k, piece in enumerate(piece_refs):
        for j in range(ranks):
            low = (j * len(piece_refs) + (at_ref[0] ^ k)) * rows
            both_ref[pl.ds(pl.multiple_of(low, rows), rows), :] = piece[at_ref[1] ^ j]
    fired, wanted = both_ref[:, :features], both_ref[:, features:]
    for part in range(3):
        in_ref[part] = dot(fired, grad_ref[part], TN)
    out_ref[...] = dot(wanted, grad_ref[3], TN)


def weight_grads(fsdp_rank, turn, pieces, grads):
    features = pieces[0].shape[2] // 2
    local = grads.shape[2]
    in_vmem = pl.BlockSpec(memory_space=pltpu.VMEM)
    return pl.pallas_call(
        weight_kernel,
        in_specs=[pl.BlockSpec(memory_space=pltpu.SMEM)] + [in_vmem] * (len(pieces) + 1),
        out_specs=[in_vmem, in_vmem],
        out_shape=[
            jax.ShapeDtypeStruct((3, features, local), F32),
            jax.ShapeDtypeStruct((features, local), F32),
        ],
        scratch_shapes=[pltpu.VMEM((grads.shape[1], 2 * features), BF16)],
        compiler_params=params(16),
        name="weight_grads",
    )(jnp.stack([fsdp_rank, turn]), *pieces, grads)


def body(tokens, positions, pulse_indicator, norm_gain, in_weight, out_weight, upstream):
    ctx, fsdp = lax.axis_size("ctx"), lax.axis_size("fsdp")
    ctx_rank, fsdp_rank = lax.axis_index("ctx"), lax.axis_index("fsdp")
    rows, model = tokens.shape
    local = out_weight.shape[0]
    share = model // fsdp
    gain = norm_gain[None, :]
    features = model // ctx
    win = jnp.transpose(in_weight, (1, 0, 2))
    payload, spikes, inv, both = project(
        fsdp_rank, ctx, tokens, pulse_indicator, gain, win, upstream, out_weight
    )
    factor, rise, fall, base, token_share = factors(
        fsdp_rank, tokens, pulse_indicator, gain, inv, upstream, share
    )

    short = ctx == 8 and fsdp == 4
    if short:
        beside = swap(payload, "ctx", 2)
        below = swap(payload, "ctx", 1)
        across = swap(payload, "ctx", 4)
        diagonal = swap(below, "ctx", 2)
        corner = swap(across, "ctx", 2)
        across_below = swap(across, "ctx", 1)
        blocks = [payload, below, beside, diagonal, across, across_below]
        blocks += [corner, swap(corner, "ctx", 1)]
        blocks[1] = pltpu.with_memory_space_constraint(below, pltpu.HBM)
        placed = jnp.concatenate(
            [lax.dynamic_slice_in_dim(positions, (ctx_rank ^ j) * rows, rows) for j in range(ctx)]
        )
        both = lax.all_to_all(after(both, below), "ctx", 0, 0)
        over = swap(both, "fsdp", 2)
        pieces = [both, swap(both, "fsdp", 1), over, swap(over, "fsdp", 1)]
        grads = attention(blocks, after(placed, over))
        own_grads = grads[:, :rows]
    else:
        grads = long_attention(lax.all_gather(payload, "ctx", axis=0, tiled=True), positions)
        own_grads = lax.dynamic_slice_in_dim(grads, ctx_rank * rows, rows, 1)
        fired, wanted = (
            lax.all_to_all(array.reshape(rows, ctx, features), "ctx", 1, 0).reshape(-1, features)
            for array in (spikes, upstream)
        )
        in_grad = jnp.stack([dot(fired, grads[part], TN) for part in range(3)])
        out_grad = dot(wanted, grads[3], TN)

    own, far, near = spread(fsdp_rank, own_grads, win, out_weight, tokens, gain, inv, factor)
    near = swap(near, "fsdp", 1)
    far = far + near[0]
    own = own + near[1]
    lines = slice(rows, rows + SUM_ROWS)
    line = own[lines] + swap(far[lines], "fsdp", 2)
    landed = swap(jnp.concatenate([far[:rows], far[rows + SUM_ROWS :]]).astype(BF16), "fsdp", 2)
    gain_grad = line[1]
    if short:
        corner_pairs = [
            (c * fsdp + f, (c ^ 1) * fsdp + (f ^ 2)) for c in range(ctx) for f in range(fsdp)
        ]
        aside = swap(own[rows + 1], "ctx", 1)
        aside = aside + lax.ppermute(far[rows + 1], ("ctx", "fsdp"), corner_pairs)
        gain_grad = gain_grad + aside
        in_grad, out_grad = weight_grads(after(fsdp_rank, gain_grad), ctx_rank, pieces, grads)
        second, third, fourth = (swap(gain_grad, "ctx", mask) for mask in (2, 4, 6))
    else:
        gain_grad = lax.psum(gain_grad, "ctx")

    grad_spikes = own[:rows] + landed[:rows].astype(F32)
    token_grad = base + (rise * grad_spikes - fall * line[0, :rows][:, None])
    projected = own[rows + SUM_ROWS :] + landed[rows:].astype(F32)
    block_out = (token_share + projected).astype(BF16)
    if short:
        third = after(third, token_grad, block_out)
        gain_grad = (gain_grad + second) + (third + fourth)
    return (block_out, token_grad, gain_grad, jnp.transpose(in_grad, (1, 0, 2)), out_grad)


def solution(mesh):
    placed = (
        P("ctx", None),
        P(),
        P(None, "ctx", None),
        P(),
        P(None, None, "fsdp"),
        P("fsdp", None),
        P("ctx", None),
    )
    return jax.shard_map(
        body,
        mesh=mesh,
        in_specs=placed,
        out_specs=(
            P("ctx", "fsdp"),
            P("ctx", "fsdp"),
            P("fsdp"),
            P("ctx", None, "fsdp"),
            P("ctx", "fsdp"),
        ),
        check_vma=False,
    )
```
